32 devices in a mesh: tm: 8 (over z, y), swath: 4 (over x, core).
Axes of the slice: x: 2, y: 2, z: 4, core: 2. Of those that a mesh axis runs over, the one named last changes fastest.
Arguments:
- design: bfloat16 [8, 2048, 512], P('tm', 'swath'), may hold values from -6 to 6
- process: bfloat16 [8, 512, 512], P('tm', 'swath')
- prior_prec: float32 [8, 512], P('tm', 'swath'), may hold values from 0.05 to 0.5
- routes: int32 [8, 16], P('tm', 'swath'), may hold values from -1 to 7, as said below
- counts: int32 [8, 4], P('tm', 'swath'), may hold values from 1 to 4
Outputs:
- reduced_diag: float32 [8, 512, 512], P('tm', 'swath')
- reduced_coupling: float32 [8, 512, 512], P('tm', 'swath')
The draws below stay inside these ranges and needn't reach their ends.
Inputs may be any that keep to these rules, and one draw needn't show every extreme that they name: `routes`: each value is the holder's own time block i or i + 1, or -1 only where i + 1 would be 8; of one holder's 4 blocks, exactly 2 name i and the others i + 1 or -1.
All inputs are finite; a program needn't handle non-finite values.
Results may differ from the reference program's by a relative error of at most 0.00073.
Values may be sent and summed in bfloat16 or wider, within the bound.
A program may use at most 64 MiB of HBM per device.

```python
import math
import jax
import jax.numpy as jnp
from jax import lax

B = 512
OBS = 128
CAP = 2
LEVELS = 3
RB = 4
NT = 8
SLOTS = 2048
N_SWATH = 4


def draw_process(key, part):
    first_key, second_key = jax.random.split(jax.random.fold_in(key, 7))
    base = jnp.exp(jax.random.uniform(first_key, (NT, B), jnp.float32, math.log(0.2), math.log(2.0)))
    noise = jax.random.normal(second_key, (NT, B, B), jnp.float32)
    outer = jnp.einsum('tij,tkj->tik', noise, noise, precision=lax.Precision.HIGHEST) / (2.0 * B)
    outer = 0.5 * (outer + jnp.swapaxes(outer, 1, 2))
    matrix = outer + base[:, :, None] * jnp.eye(B, dtype=jnp.float32)[None]
    return matrix.astype(jnp.bfloat16)


def draw_routes(key, part):
    score_key = jax.random.fold_in(key, 11)
    scores = jax.random.randint(score_key, (NT, N_SWATH, RB), 0, 1048576) * RB + jnp.arange(RB, dtype=jnp.int32)
    ranking = jnp.argsort(jnp.argsort(scores, axis=-1), axis=-1)
    ahead = (ranking >= CAP).astype(jnp.int32)
    target = jnp.arange(NT, dtype=jnp.int32)[:, None, None] + ahead
    target = jnp.where(target > NT - 1, -1, target)
    return target.reshape(NT, N_SWATH * RB).astype(jnp.int32)


def draw_counts(key, part):
    first_key, second_key, third_key = jax.random.split(jax.random.fold_in(key, 3), 3)
    values = jax.random.randint(first_key, (NT, N_SWATH), 1, RB + 1)
    row_pick = jax.random.randint(second_key, (), 1, NT)
    col_pick = jax.random.randint(third_key, (), 0, N_SWATH)
    values = values.at[row_pick, col_pick].set(RB)
    values = values.at[row_pick - 1, col_pick].set(RB)
    values = values.at[(row_pick + 1) % NT, col_pick].set(1)
    return values.astype(jnp.int32)


def block_levels(rng, extent, cuts, smallest, largest):
    def one(position, blocks):
        draws = jax.random.uniform(jax.random.fold_in(jax.random.fold_in(rng, 6), position), (blocks,), jnp.float32, smallest / len(cuts), largest / len(cuts))
        return jnp.repeat(jnp.exp(draws), extent[position] // blocks).reshape((-1,) + (1,) * (len(extent) - position - 1))

    factor_of = one(*cuts[0])
    for cut in cuts[1:]:
        factor_of = factor_of * one(*cut)
    return factor_of


def normal_values(own_key, dims, width, most, cuts=(), held_as=jnp.bfloat16):
    result = jax.random.normal(own_key, dims, jnp.float32) * width
    if len(cuts) > 0:
        result = block_levels(own_key, dims, cuts, -0.22, 0.18) * result
    return jnp.clip(result, min=-most, max=most).astype(held_as)


def setup_inputs(seed: int = 0) -> dict:
    seeds = jax.random.split(jax.random.key(seed), 6)
    design = normal_values(seeds[0], (NT, N_SWATH * RB * OBS, B), 1.0, 6.0, ((0, 8), (1, 4)))
    process = draw_process(jax.random.fold_in(seeds[5], 71), 0)
    prior_prec = jnp.clip(jnp.exp(math.log(0.5) - 2.3025851 * jax.random.uniform(seeds[2], (NT, B), jnp.float32) ** block_levels(seeds[2], (NT, B), ((0, 8), (1, 4)), -0.2, 0.2)), 0.05, 0.5)
    routes = draw_routes(jax.random.fold_in(seeds[5], 71), 0)
    counts = draw_counts(jax.random.fold_in(seeds[5], 71), 0)
    return dict(design=design, process=process, prior_prec=prior_prec, routes=routes, counts=counts)


def tri_solve(factor, right):
    return lax.linalg.triangular_solve(factor, right, left_side=True, lower=True)

def reference(design, process, prior_prec, routes, counts):
    raw_rows = design.astype(jnp.float32).reshape(NT, N_SWATH, RB, OBS, B)
    mean_sq = lax.optimization_barrier(jnp.mean(raw_rows * raw_rows, axis=-1, keepdims=True))
    scaled = raw_rows * lax.rsqrt(4.0 * SLOTS * (mean_sq + 1e-06))
    live = jnp.arange(RB)[None, None, :] < counts[:, :, None]
    target = routes.reshape(NT, N_SWATH, RB)
    time_ids = jnp.arange(NT)[:, None, None]
    to_self = live & (target == time_ids)
    to_next = live & (target == time_ids + 1)
    self_rows = jnp.where(to_self[:, :, :, None, None], scaled, 0.0).astype(jnp.bfloat16)
    next_rows = jnp.where(to_next[:, :, :, None, None], scaled, 0.0).astype(jnp.bfloat16)

    def holder_grams(pair):
        own_rows, ahead_rows = pair
        own_rows = own_rows.reshape(-1, B)
        ahead_rows = ahead_rows.reshape(-1, B)
        own_gram = lax.dot_general(own_rows.astype(jnp.float32), own_rows.astype(jnp.float32), (((0,), (0,)), ((), ())), preferred_element_type=jnp.float32)
        ahead_gram = lax.dot_general(ahead_rows.astype(jnp.float32), ahead_rows.astype(jnp.float32), (((0,), (0,)), ((), ())), preferred_element_type=jnp.float32)
        return (own_gram, ahead_gram)
    gram_self, gram_next = lax.map(holder_grams, (self_rows, next_rows))
    zero_block = jnp.zeros((1, B, B), jnp.float32)
    gram = gram_self + jnp.concatenate([zero_block, gram_next[:-1]], axis=0)
    proc = process.astype(jnp.float32)
    previous = jnp.concatenate([zero_block, proc[:-1]], axis=0)
    unit = jnp.eye(B, dtype=jnp.float32)
    diag_blocks = previous + proc + gram + prior_prec[:, :, None] * unit[None]
    coupling = -proc
    for level in range(LEVELS):
        distance = 2 ** level
        factor = jnp.linalg.cholesky(diag_blocks)
        solved = tri_solve(factor, coupling)
        eliminated = jnp.einsum('tji,tjk->tik', solved, solved, precision=lax.Precision.HIGHEST)
        zero_run = jnp.zeros((distance, B, B), jnp.float32)
        left_term = jnp.concatenate([zero_run, eliminated[:-distance]], axis=0)
        unit_run = jnp.broadcast_to(unit, (distance, B, B))
        far_factor = jnp.concatenate([factor[distance:], unit_run], axis=0)
        far_solved = jnp.concatenate([solved[distance:], zero_run], axis=0)
        has_partner = (jnp.arange(NT) + distance < NT)[:, None, None]
        cross = tri_solve(far_factor, jnp.swapaxes(coupling, 1, 2))
        right_term = jnp.einsum('tji,tjk->tik', cross, cross, precision=lax.Precision.HIGHEST)
        new_coupling = jnp.einsum('tji,tjk->tik', cross, far_solved, precision=lax.Precision.HIGHEST)
        diag_blocks = diag_blocks - left_term - jnp.where(has_partner, right_term, 0.0)
        coupling = -new_coupling
    return (diag_blocks, coupling)
```

```python
import functools

import jax
import jax.numpy as jnp
from jax import lax
from jax.experimental import pallas as pl
from jax.experimental.pallas import tpu as pltpu
from jax.sharding import PartitionSpec as P

LEVELS = 3


def passed_along(block, axis, distance):
    devices = range(lax.axis_size(axis))
    route = [(i - distance, i) for i in devices if i - distance in devices]
    return lax.ppermute(block, axis, route)


def split(x):
    high = x.astype(jnp.bfloat16)
    return high, (x - high.astype(jnp.float32)).astype(jnp.bfloat16)


def dot3(a, b, left):
    (ah, al), (bh, bl) = a, b
    dot = functools.partial(
        lax.dot_general,
        dimension_numbers=(((left,), (0,)), ((), ())),
        preferred_element_type=jnp.float32,
    )
    return dot(ah, bh) + (dot(ah, bl) + dot(al, bh))


def factor_inverse(m):
    n = m.shape[0]
    groups = n // 8
    rows = [m[8 * g : 8 * g + 8, :] for g in range(groups)]
    lane = lax.broadcasted_iota(jnp.int32, (8, n), 1)
    sub = lax.broadcasted_iota(jnp.int32, (8, n), 0)
    for j in range(n):
        g, s = divmod(j, 8)
        row = rows[g][s : s + 1, :]
        r = lax.rsqrt(row[:, j : j + 1])
        pivot_row = jnp.broadcast_to(jnp.where(lane[:1] == j, 1.0, row) * r, (8, n))
        here = lane == j
        for h in range(g, groups):
            if h == g and s == 7:
                continue
            column = rows[h][:, j : j + 1] * r
            new = jnp.where(here, 0.0, rows[h]) - column * pivot_row
            rows[h] = jnp.where(sub > s, new, rows[h]) if h == g else new
        rows[g] = jnp.where(sub == s, pivot_row, rows[g])
    out = jnp.concatenate(rows, axis=0)
    down = lax.broadcasted_iota(jnp.int32, (n, n), 0)
    across = lax.broadcasted_iota(jnp.int32, (n, n), 1)
    return jnp.where(down >= across, out, 0.0)


def level_kernel(index_ref, parts_ref, up_ref, down_ref, work, high, low):
    blocks, _, rows, order = parts_ref.shape
    wide = work.shape[2]
    for i in range(blocks):
        for part in range(3):
            work[i, :, part * order : (part + 1) * order] = parts_ref[i, part]
    for i in range(blocks):
        for k in range(i, blocks):
            here = work[i, :, k * rows : (k + 1) * rows]
            there = work[k, :, i * rows : (i + 1) * rows]
            work[i, :, k * rows : (k + 1) * rows] = 0.5 * (here + there.T)

    def step(j, carry):
        at = pl.ds(pl.multiple_of(j * rows, rows), rows)
        inverse = factor_inverse(work[j, :, at])
        solved = dot3(split(inverse), split(work[j]), 1)
        solved_high, solved_low = split(solved)
        high[at, :] = solved_high
        low[at, :] = solved_low
        for i in range(1, blocks):

            @pl.when(i > j)
            def _():
                cut = slice(i * rows, (i + 1) * rows)
                left = (high[at, cut], low[at, cut])
                work[i] = work[i] - dot3(left, (solved_high, solved_low), 0)

        return carry

    lax.fori_loop(0, blocks, step, 0)
    mine = index_ref[0] * rows
    for out_ref, base in ((up_ref, order), (down_ref, 2 * order)):
        cut = pl.ds(pl.multiple_of(base + mine, rows), rows)
        left = (high[:, cut], low[:, cut])
        for half in range(2):
            right = slice((1 + half) * order, (2 + half) * order)
            out_ref[:, half * order : (half + 1) * order] = dot3(
                left, (high[:, right], low[:, right]), 0
            )


def eliminate(index, parts):
    blocks, _, rows, order = parts.shape
    out = jax.ShapeDtypeStruct((rows, 2 * order), jnp.float32)
    return pl.pallas_call(
        level_kernel,
        out_shape=(out, out),
        in_specs=[
            pl.BlockSpec(memory_space=pltpu.SMEM),
            pl.BlockSpec(memory_space=pltpu.VMEM),
        ],
        out_specs=(pl.BlockSpec(memory_space=pltpu.VMEM),) * 2,
        scratch_shapes=[
            pltpu.VMEM((blocks, rows, 3 * order), jnp.float32),
            pltpu.VMEM((order, 3 * order), jnp.bfloat16),
            pltpu.VMEM((order, 3 * order), jnp.bfloat16),
        ],
    )(index, parts)


def slots(scaled, wanted, named, slot_count):
    place = jnp.cumsum(named.astype(jnp.int32)) - 1
    out = []
    for slot in range(slot_count):
        chosen = jnp.zeros(scaled.shape[1:], jnp.float32)
        for r in range(scaled.shape[0]):
            chosen = jnp.where(wanted[r] & (place[r] == slot), scaled[r], chosen)
        out.append(chosen)
    return jnp.concatenate(out, axis=0).astype(jnp.bfloat16)


def shards(design, process, prior_prec, routes, counts):
    row_count = process.shape[1]
    order = process.shape[2]
    my_time = lax.axis_index("tm")
    swath_index = lax.axis_index("swath")
    swath_size = lax.axis_size("swath")
    block_count = routes.shape[1]
    slot_count = block_count // 2
    block_rows = design.shape[1] // block_count
    total_slots = 2 * slot_count * block_rows * swath_size
    row_start = swath_index * row_count
    raw_rows = design[0].reshape(block_count, block_rows, order).astype(jnp.float32)
    mean_sq = jnp.mean(raw_rows * raw_rows, axis=-1, keepdims=True)
    scaled = raw_rows * lax.rsqrt(4.0 * total_slots * (mean_sq + 1e-06))
    live = jnp.arange(block_count) < counts[0, 0]
    target = routes[0]
    own, ahead = target == my_time, target == my_time + 1
    own_blocks = slots(scaled, live & own, own, slot_count)
    ahead_blocks = slots(scaled, live & ahead, ahead, slot_count)
    sent = jnp.concatenate([ahead_blocks, process[0]], axis=0)
    arrived = passed_along(sent, "tm", 1)
    prior = prior_prec[0]
    first = lax.reduce_precision(prior, 8, 7)
    second = lax.reduce_precision(prior - first, 8, 7)
    third = lax.reduce_precision(prior - first - second, 8, 7)
    pieces = jnp.zeros((16, order), jnp.float32)
    for i, piece in enumerate((first, second, third)):
        pieces = pieces.at[i, :row_count].set(piece)
    packed = jnp.concatenate(
        [own_blocks, arrived, process[0], pieces.astype(jnp.bfloat16)], axis=0
    )
    whole = lax.all_gather(packed, "swath", axis=0)
    observed = whole[:, : 2 * slot_count * block_rows].reshape(-1, order)
    cut = 2 * slot_count * block_rows
    previous = whole[:, cut : cut + row_count].reshape(order, order).astype(jnp.float32)
    cut += row_count
    current = whole[:, cut : cut + row_count].reshape(order, order).astype(jnp.float32)
    cut += row_count
    three = whole[:, cut : cut + 3, :row_count].astype(jnp.float32)
    prior_full = (three[:, 0] + three[:, 1] + three[:, 2]).reshape(order)
    gram = lax.dot_general(
        observed, observed, (((0,), (0,)), ((), ())), preferred_element_type=jnp.float32
    )
    full_diag = previous + current + gram + jnp.diag(prior_full)
    diag_rows = lax.dynamic_slice_in_dim(full_diag, row_start, row_count, 0)
    parts = jnp.stack(
        [m.reshape(swath_size, row_count, order) for m in (full_diag, current, previous.T)],
        axis=1,
    )
    index = swath_index.reshape(1).astype(jnp.int32)
    for level in range(LEVELS):
        distance = 2**level
        up, down = eliminate(index, parts)
        from_left = passed_along(up, "tm", distance)
        from_right = passed_along(down, "tm", -distance)
        diag_rows = diag_rows - from_left[:, :order] - from_right[:, order:]
        coup_rows = from_right[:, :order]
        if level < LEVELS - 1:
            mine = jnp.stack([diag_rows, coup_rows, from_left[:, order:]])
            parts = lax.all_gather(mine, "swath", axis=0)
    return (diag_rows[None], -coup_rows[None])


def solution(mesh):
    return jax.shard_map(
        shards,
        mesh=mesh,
        in_specs=(
            P("tm", "swath", None),
            P("tm", "swath", None),
            P("tm", "swath"),
            P("tm", "swath"),
            P("tm", "swath"),
        ),
        out_specs=(P("tm", "swath", None), P("tm", "swath", None)),
        check_vma=False,
    )
```

```python
import functools

import jax
import jax.numpy as jnp
from jax import lax
from jax.experimental import pallas as pl
from jax.experimental.pallas import tpu as pltpu
from jax.sharding import PartitionSpec as P

LEVELS = 3


def passed_along(block, axis, distance):
    devices = range(lax.axis_size(axis))
    route = [(i - distance, i) for i in devices if i - distance in devices]
    return lax.ppermute(block, axis, route)


def split(x):
    high = x.astype(jnp.bfloat16)
    return high, (x - high.astype(jnp.float32)).astype(jnp.bfloat16)


def dot3(a, b, left):
    (ah, al), (bh, bl) = a, b
    dot = functools.partial(
        lax.dot_general,
        dimension_numbers=(((left,), (0,)), ((), ())),
        preferred_element_type=jnp.float32,
    )
    return dot(ah, bh) + (dot(ah, bl) + dot(al, bh))


def factor_inverse(m, width=8):
    n = m.shape[0]
    groups = n // width
    rows = [m[width * g : width * (g + 1), :] for g in range(groups)]
    lane = lax.broadcasted_iota(jnp.int32, (width, n), 1)
    sub = lax.broadcasted_iota(jnp.int32, (width, n), 0)
    spread = lambda x: jnp.broadcast_to(x, (width, n))
    for g in range(groups):
        first = width * g
        inside = (lane >= first) & (lane < first + width)
        columns = {
            h: [spread(rows[h][:, first + s : first + s + 1]) for s in range(width)]
            for h in range(g, groups)
        }
        entry = {
            (k, s): spread(columns[g][s][k : k + 1, :])
            for s in range(width)
            for k in range(s, width)
        }
        solved = [
            jnp.where(lane == first + s, 1.0, jnp.where(inside, 0.0, spread(rows[g][s : s + 1, :])))
            for s in range(width)
        ]
        scale, lower = [], {}
        for s in range(width):
            scale.append(lax.rsqrt(entry[s, s]))
            solved[s] = solved[s] * scale[s]
            for k in range(s + 1, width):
                lower[k, s] = entry[k, s] * scale[s]
            for k in range(s + 1, width):
                for t in range(s + 1, k + 1):
                    entry[k, t] = entry[k, t] - lower[k, s] * lower[t, s]
                solved[k] = solved[k] - lower[k, s] * solved[s]
        back = list(solved)
        for s in range(width - 1, -1, -1):
            back[s] = back[s] * scale[s]
            for k in range(s):
                back[k] = back[k] - lower[s, k] * back[s]
        for h in range(g + 1, groups):
            left = jnp.where(inside, 0.0, rows[h])
            for s in range(width):
                left = left - columns[h][s] * back[s]
            rows[h] = left
        group = solved[0]
        for s in range(1, width):
            group = jnp.where(sub == s, solved[s], group)
        rows[g] = group
    out = jnp.concatenate(rows, axis=0)
    down = lax.broadcasted_iota(jnp.int32, (n, n), 0)
    across = lax.broadcasted_iota(jnp.int32, (n, n), 1)
    return jnp.where(down >= across, out, 0.0)


def factor_kernel(diag_ref, high, low, work):
    blocks, rows, order = diag_ref.shape
    work[...] = diag_ref[...]
    for i in range(blocks):
        for k in range(i, blocks):
            here = work[i, :, k * rows : (k + 1) * rows]
            there = work[k, :, i * rows : (i + 1) * rows]
            work[i, :, k * rows : (k + 1) * rows] = 0.5 * (here + there.T)
    down = lax.broadcasted_iota(jnp.int32, (rows, rows), 0)
    across = lax.broadcasted_iota(jnp.int32, (rows, rows), 1)
    unit = jnp.where(down == across, 1.0, 0.0)
    column_block = lax.broadcasted_iota(jnp.int32, (rows, order), 1) // rows

    def step(j, carry):
        at = pl.ds(pl.multiple_of(j * rows, rows), rows)
        inverse = factor_inverse(work[j, :, at])
        work[j, :, at] = unit
        solved = dot3(split(inverse), split(work[j]), 1)
        solved_high, solved_low = split(solved)
        high[at, :] = solved_high
        low[at, :] = solved_low
        for i in range(1, blocks):

            @pl.when(i > j)
            def _():
                cut = slice(i * rows, (i + 1) * rows)
                left = (high[at, cut], low[at, cut])
                work[i, :, at] = jnp.zeros((rows, rows), jnp.float32)
                work[i] = work[i] - dot3(left, (solved_high, solved_low), 0)

        keep = column_block <= j
        high[at, :] = jnp.where(keep, solved_high, 0.0).astype(jnp.bfloat16)
        low[at, :] = jnp.where(keep, solved_low, 0.0).astype(jnp.bfloat16)
        return carry

    lax.fori_loop(0, blocks, step, 0)


def factor(diag):
    blocks, rows, order = diag.shape
    out = jax.ShapeDtypeStruct((order, order), jnp.bfloat16)
    return pl.pallas_call(
        factor_kernel,
        out_shape=(out, out),
        in_specs=[pl.BlockSpec(memory_space=pltpu.VMEM)],
        out_specs=(pl.BlockSpec(memory_space=pltpu.VMEM),) * 2,
        scratch_shapes=[pltpu.VMEM((blocks, rows, order), jnp.float32)],
        cost_estimate=pl.CostEstimate(flops=20000000000, bytes_accessed=4 * order * order, transcendentals=0),
    )(diag)


def term_kernel(index_ref, inverse_high, inverse_low, parts_ref, out_ref, high, low):
    blocks, _, rows, order = parts_ref.shape
    for part in range(2):
        across = slice(part * order, (part + 1) * order)
        right = [split(parts_ref[i, part]) for i in range(blocks)]
        right = [jnp.concatenate([r[k] for r in right], axis=0) for k in range(2)]
        for j in range(blocks):
            at, deep = slice(j * rows, (j + 1) * rows), (j + 1) * rows
            left = (inverse_high[at, :deep], inverse_low[at, :deep])
            solved = dot3(left, (right[0][:deep], right[1][:deep]), 1)
            solved_high, solved_low = split(solved)
            high[at, across] = solved_high
            low[at, across] = solved_low
    mine = index_ref[0] * rows
    for k, (first, second) in enumerate(((0, 0), (0, 1), (1, 1), (1, 0))):
        cut = pl.ds(pl.multiple_of(first * order + mine, rows), rows)
        across = slice(second * order, (second + 1) * order)
        out_ref[k] = dot3((high[:, cut], low[:, cut]), (high[:, across], low[:, across]), 0)


def terms(index, inverse, parts):
    blocks, _, rows, order = parts.shape
    return pl.pallas_call(
        term_kernel,
        out_shape=jax.ShapeDtypeStruct((4, rows, order), jnp.float32),
        in_specs=[pl.BlockSpec(memory_space=pltpu.SMEM)]
        + [pl.BlockSpec(memory_space=pltpu.VMEM)] * 3,
        out_specs=pl.BlockSpec(memory_space=pltpu.VMEM),
        scratch_shapes=[pltpu.VMEM((order, 2 * order), jnp.bfloat16)] * 2,
        cost_estimate=pl.CostEstimate(flops=4000000000, bytes_accessed=16 * order * order, transcendentals=0),
    )(index, *inverse, parts)


def slots(scaled, wanted, named, slot_count):
    place = jnp.cumsum(named.astype(jnp.int32)) - 1
    out = []
    for slot in range(slot_count):
        chosen = jnp.zeros(scaled.shape[1:], jnp.float32)
        for r in range(scaled.shape[0]):
            chosen = jnp.where(wanted[r] & (place[r] == slot), scaled[r], chosen)
        out.append(chosen)
    return jnp.concatenate(out, axis=0).astype(jnp.bfloat16)


def shards(design, process, prior_prec, routes, counts):
    row_count = process.shape[1]
    order = process.shape[2]
    my_time = lax.axis_index("tm")
    swath_index = lax.axis_index("swath")
    swath_size = lax.axis_size("swath")
    block_count = routes.shape[1]
    slot_count = block_count // 2
    block_rows = design.shape[1] // block_count
    total_slots = 2 * slot_count * block_rows * swath_size
    row_start = swath_index * row_count
    raw_rows = design[0].reshape(block_count, block_rows, order).astype(jnp.float32)
    mean_sq = jnp.mean(raw_rows * raw_rows, axis=-1, keepdims=True)
    scaled = raw_rows * lax.rsqrt(4.0 * total_slots * (mean_sq + 1e-06))
    live = jnp.arange(block_count) < counts[0, 0]
    target = routes[0]
    own, ahead = target == my_time, target == my_time + 1
    own_blocks = slots(scaled, live & own, own, slot_count)
    ahead_blocks = slots(scaled, live & ahead, ahead, slot_count)
    sent = jnp.concatenate([ahead_blocks, process[0]], axis=0)
    arrived = passed_along(sent, "tm", 1)
    prior = prior_prec[0]
    first = lax.reduce_precision(prior, 8, 7)
    second = lax.reduce_precision(prior - first, 8, 7)
    third = lax.reduce_precision(prior - first - second, 8, 7)
    pieces = jnp.zeros((16, order), jnp.float32)
    for i, piece in enumerate((first, second, third)):
        pieces = pieces.at[i, :row_count].set(piece)
    near = jnp.concatenate([own_blocks, process[0], pieces.astype(jnp.bfloat16)], axis=0)
    near = lax.all_gather(near, "swath", axis=0)
    far = lax.all_gather(arrived, "swath", axis=0)
    cut = slot_count * block_rows
    over_rows = lambda w: lax.dot_general(
        w, w, (((0,), (0,)), ((), ())), preferred_element_type=jnp.float32
    )
    previous = far[:, cut:].reshape(order, order).astype(jnp.float32)
    current = near[:, cut : cut + row_count].reshape(order, order).astype(jnp.float32)
    three = near[:, cut + row_count : cut + row_count + 3, :row_count].astype(jnp.float32)
    prior_full = (three[:, 0] + three[:, 1] + three[:, 2]).reshape(order)
    gram = over_rows(near[:, :cut].reshape(-1, order)) + over_rows(far[:, :cut].reshape(-1, order))
    full_diag = previous + current + gram + jnp.diag(prior_full)
    diag_rows = lax.dynamic_slice_in_dim(full_diag, row_start, row_count, 0)
    full_diag = full_diag.reshape(swath_size, row_count, order)
    parts = jnp.stack(
        [m.reshape(swath_size, row_count, order) for m in (current, previous.T)], axis=1
    )
    index = swath_index.reshape(1).astype(jnp.int32)
    for level in range(LEVELS):
        distance = 2**level
        out = terms(index, factor(full_diag), parts)
        left_term = passed_along(out[0], "tm", distance)
        right_term = passed_along(out[2], "tm", -distance)
        diag_rows = diag_rows - left_term - right_term
        if level < LEVELS - 1:
            diag_rows, across, back = lax.optimization_barrier((diag_rows, out[1], out[3]))
            full_diag = lax.all_gather(diag_rows, "swath", axis=0)
            ahead = passed_along(across, "tm", distance)
            coup_rows = passed_along(back, "tm", -distance)
            full_diag, ahead, coup_rows = lax.optimization_barrier((full_diag, ahead, coup_rows))
            parts = lax.all_gather(jnp.stack([coup_rows, ahead]), "swath", axis=0)
        else:
            coup_rows = passed_along(out[3], "tm", -distance)
    return (diag_rows[None], -coup_rows[None])


def solution(mesh):
    return jax.shard_map(
        shards,
        mesh=mesh,
        in_specs=(
            P("tm", "swath", None),
            P("tm", "swath", None),
            P("tm", "swath"),
            P("tm", "swath"),
            P("tm", "swath"),
        ),
        out_specs=(P("tm", "swath", None), P("tm", "swath", None)),
        check_vma=False,
    )
```

```python
import functools

import jax
import jax.numpy as jnp
from jax import lax
from jax.experimental import pallas as pl
from jax.experimental.pallas import tpu as pltpu
from jax.sharding import PartitionSpec as P

LEVELS = 3


def passed_along(block, axis, distance):
    devices = range(lax.axis_size(axis))
    route = [(i - distance, i) for i in devices if i - distance in devices]
    return lax.ppermute(block, axis, route)


def split(x):
    high = x.astype(jnp.bfloat16)
    return high, (x - high.astype(jnp.float32)).astype(jnp.bfloat16)


def dot3(a, b, left):
    (ah, al), (bh, bl) = a, b
    dot = functools.partial(
        lax.dot_general,
        dimension_numbers=(((left,), (0,)), ((), ())),
        preferred_element_type=jnp.float32,
    )
    return dot(ah, bh) + (dot(ah, bl) + dot(al, bh))


def factor_inverse(m, width=8):
    n = m.shape[0]
    groups = n // width
    rows = [m[width * g : width * (g + 1), :] for g in range(groups)]
    lane = lax.broadcasted_iota(jnp.int32, (width, n), 1)
    sub = lax.broadcasted_iota(jnp.int32, (width, n), 0)
    spread = lambda x: jnp.broadcast_to(x, (width, n))
    for g in range(groups):
        first = width * g
        inside = (lane >= first) & (lane < first + width)
        columns = {
            h: [spread(rows[h][:, first + s : first + s + 1]) for s in range(width)]
            for h in range(g, groups)
        }
        entry = {
            (k, s): spread(columns[g][s][k : k + 1, :])
            for s in range(width)
            for k in range(s, width)
        }
        solved = [
            jnp.where(lane == first + s, 1.0, jnp.where(inside, 0.0, spread(rows[g][s : s + 1, :])))
            for s in range(width)
        ]
        scale, lower = [], {}
        for s in range(width):
            scale.append(lax.rsqrt(entry[s, s]))
            solved[s] = solved[s] * scale[s]
            for k in range(s + 1, width):
                lower[k, s] = entry[k, s] * scale[s]
            for k in range(s + 1, width):
                for t in range(s + 1, k + 1):
                    entry[k, t] = entry[k, t] - lower[k, s] * lower[t, s]
                solved[k] = solved[k] - lower[k, s] * solved[s]
        back = list(solved)
        for s in range(width - 1, -1, -1):
            back[s] = back[s] * scale[s]
            for k in range(s):
                back[k] = back[k] - lower[s, k] * back[s]
        for h in range(g + 1, groups):
            left = jnp.where(inside, 0.0, rows[h])
            for s in range(width):
                left = left - columns[h][s] * back[s]
            rows[h] = left
        group = solved[0]
        for s in range(1, width):
            group = jnp.where(sub == s, solved[s], group)
        rows[g] = group
    out = jnp.concatenate(rows, axis=0)
    down = lax.broadcasted_iota(jnp.int32, (n, n), 0)
    across = lax.broadcasted_iota(jnp.int32, (n, n), 1)
    return jnp.where(down >= across, out, 0.0)


def factor_kernel(diag_ref, high, low, work, beside=None):
    blocks, rows, order = diag_ref.shape
    work[...] = diag_ref[...]
    for i in range(blocks):
        for k in range(i, blocks):
            here = work[i, :, k * rows : (k + 1) * rows]
            there = work[k, :, i * rows : (i + 1) * rows]
            work[i, :, k * rows : (k + 1) * rows] = 0.5 * (here + there.T)
    down = lax.broadcasted_iota(jnp.int32, (rows, rows), 0)
    across = lax.broadcasted_iota(jnp.int32, (rows, rows), 1)
    unit = jnp.where(down == across, 1.0, 0.0)
    column_block = lax.broadcasted_iota(jnp.int32, (rows, order), 1) // rows

    def step(j, carry):
        at = pl.ds(pl.multiple_of(j * rows, rows), rows)
        if beside is not None:
            beside(j)
        inverse = factor_inverse(work[j, :, at])
        work[j, :, at] = unit
        solved = dot3(split(inverse), split(work[j]), 1)
        solved_high, solved_low = split(solved)
        high[at, :] = solved_high
        low[at, :] = solved_low
        for i in range(1, blocks):

            @pl.when(i > j)
            def _():
                cut = slice(i * rows, (i + 1) * rows)
                left = (high[at, cut], low[at, cut])
                work[i, :, at] = jnp.zeros((rows, rows), jnp.float32)
                work[i] = work[i] - dot3(left, (solved_high, solved_low), 0)

        keep = column_block <= j
        high[at, :] = jnp.where(keep, solved_high, 0.0).astype(jnp.bfloat16)
        low[at, :] = jnp.where(keep, solved_low, 0.0).astype(jnp.bfloat16)
        return carry

    lax.fori_loop(0, blocks, step, 0)


def factor(diag):
    blocks, rows, order = diag.shape
    out = jax.ShapeDtypeStruct((order, order), jnp.bfloat16)
    return pl.pallas_call(
        factor_kernel,
        out_shape=(out, out),
        in_specs=[pl.BlockSpec(memory_space=pltpu.VMEM)],
        out_specs=(pl.BlockSpec(memory_space=pltpu.VMEM),) * 2,
        scratch_shapes=[pltpu.VMEM((blocks, rows, order), jnp.float32)],
        cost_estimate=pl.CostEstimate(flops=20000000000, bytes_accessed=4 * order * order, transcendentals=0),
    )(diag)


def term_kernel(index_ref, inverse_high, inverse_low, parts_ref, out_ref, high, low):
    put_terms(index_ref[0], inverse_high, inverse_low, parts_ref, out_ref, high, low)


def put_terms(index, inverse_high, inverse_low, parts_ref, out_ref, high, low):
    blocks, _, rows, order = parts_ref.shape
    for part in range(2):
        across = slice(part * order, (part + 1) * order)
        right = [split(parts_ref[i, part]) for i in range(blocks)]
        right = [jnp.concatenate([r[k] for r in right], axis=0) for k in range(2)]
        for j in range(blocks):
            at, deep = slice(j * rows, (j + 1) * rows), (j + 1) * rows
            left = (inverse_high[at, :deep], inverse_low[at, :deep])
            solved = dot3(left, (right[0][:deep], right[1][:deep]), 1)
            solved_high, solved_low = split(solved)
            high[at, across] = solved_high
            low[at, across] = solved_low
    mine = index * rows
    for k, (first, second) in enumerate(((0, 0), (0, 1), (1, 1), (1, 0))):
        cut = pl.ds(pl.multiple_of(first * order + mine, rows), rows)
        across = slice(second * order, (second + 1) * order)
        out_ref[k] = dot3((high[:, cut], low[:, cut]), (high[:, across], low[:, across]), 0)


def terms(index, inverse, parts):
    blocks, _, rows, order = parts.shape
    return pl.pallas_call(
        term_kernel,
        out_shape=jax.ShapeDtypeStruct((4, rows, order), jnp.float32),
        in_specs=[pl.BlockSpec(memory_space=pltpu.SMEM)]
        + [pl.BlockSpec(memory_space=pltpu.VMEM)] * 3,
        out_specs=pl.BlockSpec(memory_space=pltpu.VMEM),
        scratch_shapes=[pltpu.VMEM((order, 2 * order), jnp.bfloat16)] * 2,
        cost_estimate=pl.CostEstimate(flops=4000000000, bytes_accessed=16 * order * order, transcendentals=0),
    )(index, *inverse, parts)


MESH = pl.DeviceIdType.MESH


def across(place, bit):
    return place + bit - 2 * bit * ((place // bit) % 2)


class Spread:
    def __init__(self, size, place, block, send_sem, recv_sem):
        bits = [size >> (k + 1) for k in range(size.bit_length() - 1)]
        self.plan = [(b, 0) for b in bits]
        for k, b in enumerate(bits):
            earlier = [0]
            for e in bits[:k]:
                earlier += [m + e for m in earlier]
            self.plan += [(b, m) for m in earlier if m]
        self.copies, self.arrived = [], set()
        for k, (b, m) in enumerate(self.plan):
            held = place
            for e in bits:
                if m & e:
                    held = across(held, e)
            self.copies.append(
                pltpu.make_async_remote_copy(
                    src_ref=block.at[held],
                    dst_ref=block.at[held],
                    send_sem=send_sem.at[k],
                    recv_sem=recv_sem.at[k],
                    device_id={"swath": across(place, b)},
                    device_id_type=MESH,
                )
            )

    def start_own(self):
        for copy, (b, m) in zip(self.copies, self.plan):
            if m == 0:
                copy.start()

    def forward(self):
        for copy, (b, m) in zip(self.copies, self.plan):
            if m:
                last = m & -m
                source = self.plan.index((last, m - last))
                if source not in self.arrived:
                    self.copies[source].wait_recv()
                    self.arrived.add(source)
                copy.start()

    def finish(self):
        for k, copy in enumerate(self.copies):
            if k not in self.arrived:
                copy.wait_recv()
        for copy in self.copies:
            copy.wait_send()


def greet(distance, times, size, spread_too):
    place, me = lax.axis_index("swath"), lax.axis_index("tm")
    barrier = pltpu.get_barrier_semaphore()
    behind, ahead = me >= distance, me + distance < times

    @pl.when(behind)
    def _():
        pl.semaphore_signal(barrier, inc=1, device_id={"tm": me - distance}, device_id_type=MESH)

    @pl.when(ahead)
    def _():
        pl.semaphore_signal(barrier, inc=1, device_id={"tm": me + distance}, device_id_type=MESH)

    count = behind.astype(jnp.int32) + ahead.astype(jnp.int32)
    if spread_too:
        bits = [size >> (k + 1) for k in range(size.bit_length() - 1)]
        for b in bits:
            pl.semaphore_signal(
                barrier, inc=1, device_id={"swath": across(place, b)}, device_id_type=MESH
            )
        count = count + len(bits)
    pl.semaphore_wait(barrier, count)
    return place, me, behind, ahead


def handed(me, distance, behind, ahead, moves, send_sem, recv_sem):
    plan = []
    for k, (source, target, up) in enumerate(moves):
        copy = pltpu.make_async_remote_copy(
            src_ref=source,
            dst_ref=target,
            send_sem=send_sem.at[k],
            recv_sem=recv_sem.at[k],
            device_id={"tm": me + distance if up else me - distance},
            device_id_type=MESH,
        )
        plan.append((copy, target, ahead if up else behind, behind if up else ahead))

    def start(items):
        for copy, target, sends, receives in items:
            pl.when(sends)(copy.start)

    def receive(items):
        for copy, target, sends, receives in items:
            pl.when(receives)(copy.wait_recv)

            @pl.when(jnp.logical_not(receives))
            def _():
                target[...] = jnp.zeros(target.shape, target.dtype)

    def sent(items):
        for copy, target, sends, receives in items:
            pl.when(sends)(copy.wait_send)

    return plan, start, receive, sent


def step_kernel(distance, times, size, terms_ref, diag_ref, out_ref, out_diag_ref, land, diag_full,
                parts, high, low, work, solved_high, solved_low, move_send, move_recv,
                diag_send, diag_recv, part_send, part_recv):
    place, me, behind, ahead = greet(distance, times, size, True)
    moves = [
        (terms_ref.at[0], land.at[0], True),
        (terms_ref.at[2], land.at[1], False),
        (terms_ref.at[3], parts.at[place, 0], False),
        (terms_ref.at[1], parts.at[place, 1], True),
    ]
    plan, start, receive, sent = handed(
        me, distance, behind, ahead, moves, move_send, move_recv
    )
    start(plan)
    receive(plan[:2])
    mine = diag_ref[...] - land[0] - land[1]
    out_diag_ref[...] = mine
    diag_full[place] = mine
    spread = Spread(size, place, diag_full, diag_send, diag_recv)
    spread.start_own()
    spread.forward()
    spread.finish()
    part_spread = Spread(size, place, parts, part_send, part_recv)
    blocks = diag_full.shape[0]

    def beside(j):
        @pl.when(j == 1)
        def _():
            receive(plan[2:])
            part_spread.start_own()

        @pl.when(j == blocks - 1)
        def _():
            part_spread.forward()

    factor_kernel(diag_full, high, low, work, beside)
    part_spread.finish()
    sent(plan)
    put_terms(place, high, low, parts, out_ref, solved_high, solved_low)


def step(distance, terms_in, diag_rows):
    times, size = lax.axis_size("tm"), lax.axis_size("swath")
    rows, order = diag_rows.shape
    vmem = pl.BlockSpec(memory_space=pltpu.VMEM)
    dma = pltpu.SemaphoreType.DMA
    return pl.pallas_call(
        functools.partial(step_kernel, distance, times, size),
        out_shape=(
            jax.ShapeDtypeStruct((4, rows, order), jnp.float32),
            jax.ShapeDtypeStruct((rows, order), jnp.float32),
        ),
        in_specs=[vmem] * 2,
        out_specs=(vmem,) * 2,
        scratch_shapes=[
            pltpu.VMEM((2, rows, order), jnp.float32),
            pltpu.VMEM((size, rows, order), jnp.float32),
            pltpu.VMEM((size, 2, rows, order), jnp.float32),
            pltpu.VMEM((order, order), jnp.bfloat16),
            pltpu.VMEM((order, order), jnp.bfloat16),
            pltpu.VMEM((size, rows, order), jnp.float32),
            pltpu.VMEM((order, 2 * order), jnp.bfloat16),
            pltpu.VMEM((order, 2 * order), jnp.bfloat16),
            dma((4,)),
            dma((4,)),
            dma((size - 1,)),
            dma((size - 1,)),
            dma((size - 1,)),
            dma((size - 1,)),
        ],
        compiler_params=pltpu.CompilerParams(collective_id=distance, has_side_effects=True),
    )(terms_in, diag_rows)


def last_kernel(distance, times, size, terms_ref, diag_ref, out_diag_ref, out_coup_ref, land, move_send, move_recv):
    place, me, behind, ahead = greet(distance, times, size, False)
    moves = [
        (terms_ref.at[3], land.at[2], False),
        (terms_ref.at[0], land.at[0], True),
        (terms_ref.at[2], land.at[1], False),
    ]
    plan, start, receive, sent = handed(
        me, distance, behind, ahead, moves, move_send, move_recv
    )
    start(plan)
    receive(plan)
    out_coup_ref[...] = -land[2]
    out_diag_ref[...] = diag_ref[...] - land[0] - land[1]
    sent(plan)


def last(distance, terms_in, diag_rows):
    times, size = lax.axis_size("tm"), lax.axis_size("swath")
    rows, order = diag_rows.shape
    vmem = pl.BlockSpec(memory_space=pltpu.VMEM)
    return pl.pallas_call(
        functools.partial(last_kernel, distance, times, size),
        out_shape=(jax.ShapeDtypeStruct((rows, order), jnp.float32),) * 2,
        in_specs=[vmem] * 2,
        out_specs=(vmem,) * 2,
        scratch_shapes=[
            pltpu.VMEM((3, rows, order), jnp.float32),
            pltpu.SemaphoreType.DMA((3,)),
            pltpu.SemaphoreType.DMA((3,)),
        ],
        compiler_params=pltpu.CompilerParams(collective_id=distance, has_side_effects=True),
    )(terms_in, diag_rows)


def slots(scaled, wanted, named, slot_count):
    place = jnp.cumsum(named.astype(jnp.int32)) - 1
    out = []
    for slot in range(slot_count):
        chosen = jnp.zeros(scaled.shape[1:], jnp.float32)
        for r in range(scaled.shape[0]):
            chosen = jnp.where(wanted[r] & (place[r] == slot), scaled[r], chosen)
        out.append(chosen)
    return jnp.concatenate(out, axis=0).astype(jnp.bfloat16)


def shards(design, process, prior_prec, routes, counts):
    row_count = process.shape[1]
    order = process.shape[2]
    my_time = lax.axis_index("tm")
    swath_index = lax.axis_index("swath")
    swath_size = lax.axis_size("swath")
    block_count = routes.shape[1]
    slot_count = block_count // 2
    block_rows = design.shape[1] // block_count
    total_slots = 2 * slot_count * block_rows * swath_size
    row_start = swath_index * row_count
    raw_rows = design[0].reshape(block_count, block_rows, order).astype(jnp.float32)
    mean_sq = jnp.mean(raw_rows * raw_rows, axis=-1, keepdims=True)
    scaled = raw_rows * lax.rsqrt(4.0 * total_slots * (mean_sq + 1e-06))
    live = jnp.arange(block_count) < counts[0, 0]
    target = routes[0]
    own, ahead = target == my_time, target == my_time + 1
    own_blocks = slots(scaled, live & own, own, slot_count)
    ahead_blocks = slots(scaled, live & ahead, ahead, slot_count)
    sent = jnp.concatenate([ahead_blocks, process[0]], axis=0)
    arrived = passed_along(sent, "tm", 1)
    prior = prior_prec[0]
    first = lax.reduce_precision(prior, 8, 7)
    second = lax.reduce_precision(prior - first, 8, 7)
    third = lax.reduce_precision(prior - first - second, 8, 7)
    pieces = jnp.zeros((16, order), jnp.float32)
    for i, piece in enumerate((first, second, third)):
        pieces = pieces.at[i, :row_count].set(piece)
    near = jnp.concatenate([own_blocks, process[0], pieces.astype(jnp.bfloat16)], axis=0)
    near = lax.all_gather(near, "swath", axis=0)
    far = lax.all_gather(arrived, "swath", axis=0)
    cut = slot_count * block_rows
    over_rows = lambda w: lax.dot_general(
        w, w, (((0,), (0,)), ((), ())), preferred_element_type=jnp.float32
    )
    previous = far[:, cut:].reshape(order, order).astype(jnp.float32)
    current = near[:, cut : cut + row_count].reshape(order, order).astype(jnp.float32)
    three = near[:, cut + row_count : cut + row_count + 3, :row_count].astype(jnp.float32)
    prior_full = (three[:, 0] + three[:, 1] + three[:, 2]).reshape(order)
    gram = over_rows(near[:, :cut].reshape(-1, order)) + over_rows(far[:, :cut].reshape(-1, order))
    full_diag = previous + current + gram + jnp.diag(prior_full)
    diag_rows = lax.dynamic_slice_in_dim(full_diag, row_start, row_count, 0)
    full_diag = full_diag.reshape(swath_size, row_count, order)
    parts = jnp.stack(
        [m.reshape(swath_size, row_count, order) for m in (current, previous.T)], axis=1
    )
    index = swath_index.reshape(1).astype(jnp.int32)
    out = terms(index, factor(full_diag), parts)
    for level in range(LEVELS - 1):
        out, diag_rows = step(2**level, out, diag_rows)
    diag_rows, coup_rows = last(2 ** (LEVELS - 1), out, diag_rows)
    return (diag_rows[None], coup_rows[None])


def solution(mesh):
    return jax.shard_map(
        shards,
        mesh=mesh,
        in_specs=(
            P("tm", "swath", None),
            P("tm", "swath", None),
            P("tm", "swath"),
            P("tm", "swath"),
            P("tm", "swath"),
        ),
        out_specs=(P("tm", "swath", None), P("tm", "swath", None)),
        check_vma=False,
    )
```

```python
import functools

import jax
import jax.numpy as jnp
from jax import lax
from jax.experimental import pallas as pl
from jax.experimental.pallas import tpu as pltpu
from jax.sharding import PartitionSpec as P

LEVELS = 3


def split(x):
    high = x.astype(jnp.bfloat16)
    return high, (x - high.astype(jnp.float32)).astype(jnp.bfloat16)


def dot3(a, b, left):
    (ah, al), (bh, bl) = a, b
    dot = functools.partial(
        lax.dot_general,
        dimension_numbers=(((left,), (0,)), ((), ())),
        preferred_element_type=jnp.float32,
    )
    return dot(ah, bh) + (dot(ah, bl) + dot(al, bh))


def factor_inverse(m, width=8):
    n = m.shape[0]
    groups = n // width
    rows = [m[width * g : width * (g + 1), :] for g in range(groups)]
    lane = lax.broadcasted_iota(jnp.int32, (width, n), 1)
    sub = lax.broadcasted_iota(jnp.int32, (width, n), 0)
    spread = lambda x: jnp.broadcast_to(x, (width, n))
    for g in range(groups):
        first = width * g
        inside = (lane >= first) & (lane < first + width)
        columns = {
            h: [spread(rows[h][:, first + s : first + s + 1]) for s in range(width)]
            for h in range(g, groups)
        }
        entry = {
            (k, s): spread(columns[g][s][k : k + 1, :])
            for s in range(width)
            for k in range(s, width)
        }
        solved = [
            jnp.where(lane == first + s, 1.0, jnp.where(inside, 0.0, spread(rows[g][s : s + 1, :])))
            for s in range(width)
        ]
        scale, lower = [], {}
        for s in range(width):
            scale.append(lax.rsqrt(entry[s, s]))
            solved[s] = solved[s] * scale[s]
            for k in range(s + 1, width):
                lower[k, s] = entry[k, s] * scale[s]
            for k in range(s + 1, width):
                for t in range(s + 1, k + 1):
                    entry[k, t] = entry[k, t] - lower[k, s] * lower[t, s]
                solved[k] = solved[k] - lower[k, s] * solved[s]
        back = list(solved)
        for s in range(width - 1, -1, -1):
            back[s] = back[s] * scale[s]
            for k in range(s):
                back[k] = back[k] - lower[s, k] * back[s]
        for h in range(g + 1, groups):
            left = jnp.where(inside, 0.0, rows[h])
            for s in range(width):
                left = left - columns[h][s] * back[s]
            rows[h] = left
        group = solved[0]
        for s in range(1, width):
            group = jnp.where(sub == s, solved[s], group)
        rows[g] = group
    out = jnp.concatenate(rows, axis=0)
    down = lax.broadcasted_iota(jnp.int32, (n, n), 0)
    across = lax.broadcasted_iota(jnp.int32, (n, n), 1)
    return jnp.where(down >= across, out, 0.0)


def factor_kernel(diag_ref, high, low, work, beside=None):
    blocks, rows, order = diag_ref.shape
    work[...] = diag_ref[...]
    for i in range(blocks):
        for k in range(i, blocks):
            here = work[i, :, k * rows : (k + 1) * rows]
            there = work[k, :, i * rows : (i + 1) * rows]
            work[i, :, k * rows : (k + 1) * rows] = 0.5 * (here + there.T)
    down = lax.broadcasted_iota(jnp.int32, (rows, rows), 0)
    across = lax.broadcasted_iota(jnp.int32, (rows, rows), 1)
    unit = jnp.where(down == across, 1.0, 0.0)
    column_block = lax.broadcasted_iota(jnp.int32, (rows, order), 1) // rows

    def step(j, carry):
        at = pl.ds(pl.multiple_of(j * rows, rows), rows)
        if beside is not None:
            beside(j)
        inverse = factor_inverse(work[j, :, at])
        work[j, :, at] = unit
        solved = dot3(split(inverse), split(work[j]), 1)
        solved_high, solved_low = split(solved)
        high[at, :] = solved_high
        low[at, :] = solved_low
        for i in range(1, blocks):

            @pl.when(i > j)
            def _():
                cut = slice(i * rows, (i + 1) * rows)
                left = (high[at, cut], low[at, cut])
                work[i, :, at] = jnp.zeros((rows, rows), jnp.float32)
                work[i] = work[i] - dot3(left, (solved_high, solved_low), 0)

        keep = column_block <= j
        high[at, :] = jnp.where(keep, solved_high, 0.0).astype(jnp.bfloat16)
        low[at, :] = jnp.where(keep, solved_low, 0.0).astype(jnp.bfloat16)
        return carry

    lax.fori_loop(0, blocks, step, 0)


def put_terms(index, inverse_high, inverse_low, parts_ref, out_ref, high, low):
    blocks, _, rows, order = parts_ref.shape
    for part in range(2):
        across = slice(part * order, (part + 1) * order)
        right = [split(parts_ref[i, part]) for i in range(blocks)]
        right = [jnp.concatenate([r[k] for r in right], axis=0) for k in range(2)]
        for j in range(blocks):
            at, deep = slice(j * rows, (j + 1) * rows), (j + 1) * rows
            left = (inverse_high[at, :deep], inverse_low[at, :deep])
            solved = dot3(left, (right[0][:deep], right[1][:deep]), 1)
            solved_high, solved_low = split(solved)
            high[at, across] = solved_high
            low[at, across] = solved_low
    mine = index * rows
    for k, (first, second) in enumerate(((0, 0), (0, 1), (1, 1), (1, 0))):
        cut = pl.ds(pl.multiple_of(first * order + mine, rows), rows)
        across = slice(second * order, (second + 1) * order)
        out_ref[k] = dot3((high[:, cut], low[:, cut]), (high[:, across], low[:, across]), 0)


MESH = pl.DeviceIdType.MESH


def across(place, bit):
    return place + bit - 2 * bit * ((place // bit) % 2)


class Spread:
    def __init__(self, size, place, block, send_sem, recv_sem, own=None):
        bits = [size >> (k + 1) for k in range(size.bit_length() - 1)]
        self.plan = [(b, 0) for b in bits]
        for k, b in enumerate(bits):
            earlier = [0]
            for e in bits[:k]:
                earlier += [m + e for m in earlier]
            self.plan += [(b, m) for m in earlier if m]
        self.copies, self.arrived = [], set()
        for k, (b, m) in enumerate(self.plan):
            held = place
            for e in bits:
                if m & e:
                    held = across(held, e)
            self.copies.append(
                pltpu.make_async_remote_copy(
                    src_ref=own if own is not None and m == 0 else block.at[held],
                    dst_ref=block.at[held],
                    send_sem=send_sem.at[k],
                    recv_sem=recv_sem.at[k],
                    device_id={"swath": across(place, b)},
                    device_id_type=MESH,
                )
            )

    def start_own(self):
        for copy, (b, m) in zip(self.copies, self.plan):
            if m == 0:
                copy.start()

    def forward(self):
        for copy, (b, m) in zip(self.copies, self.plan):
            if m:
                last = m & -m
                source = self.plan.index((last, m - last))
                if source not in self.arrived:
                    self.copies[source].wait_recv()
                    self.arrived.add(source)
                copy.start()

    def finish(self):
        for k, copy in enumerate(self.copies):
            if k not in self.arrived:
                copy.wait_recv()
        for copy in self.copies:
            copy.wait_send()


def greet(distance, times, size, spread_too):
    place, me = lax.axis_index("swath"), lax.axis_index("tm")
    barrier = pltpu.get_barrier_semaphore()
    behind, ahead = me >= distance, me + distance < times

    @pl.when(behind)
    def _():
        pl.semaphore_signal(barrier, inc=1, device_id={"tm": me - distance}, device_id_type=MESH)

    @pl.when(ahead)
    def _():
        pl.semaphore_signal(barrier, inc=1, device_id={"tm": me + distance}, device_id_type=MESH)

    count = behind.astype(jnp.int32) + ahead.astype(jnp.int32)
    if spread_too:
        bits = [size >> (k + 1) for k in range(size.bit_length() - 1)]
        for b in bits:
            pl.semaphore_signal(
                barrier, inc=1, device_id={"swath": across(place, b)}, device_id_type=MESH
            )
        count = count + len(bits)
    pl.semaphore_wait(barrier, count)
    return place, me, behind, ahead


def handed(me, distance, behind, ahead, moves, send_sem, recv_sem):
    plan = []
    for k, (source, target, up) in enumerate(moves):
        copy = pltpu.make_async_remote_copy(
            src_ref=source,
            dst_ref=target,
            send_sem=send_sem.at[k],
            recv_sem=recv_sem.at[k],
            device_id={"tm": me + distance if up else me - distance},
            device_id_type=MESH,
        )
        plan.append((copy, target, ahead if up else behind, behind if up else ahead))

    def start(items):
        for copy, target, sends, receives in items:
            pl.when(sends)(copy.start)

    def receive(items):
        for copy, target, sends, receives in items:
            pl.when(receives)(copy.wait_recv)

            @pl.when(jnp.logical_not(receives))
            def _():
                target[...] = jnp.zeros(target.shape, target.dtype)

    def sent(items):
        for copy, target, sends, receives in items:
            pl.when(sends)(copy.wait_send)

    return plan, start, receive, sent


def step_kernel(distance, times, size, terms_ref, diag_ref, out_ref, out_diag_ref, land, diag_full,
                parts, high, low, work, solved_high, solved_low, move_send, move_recv,
                diag_send, diag_recv, part_send, part_recv):
    place, me, behind, ahead = greet(distance, times, size, True)
    moves = [
        (terms_ref.at[0], land.at[0], True),
        (terms_ref.at[2], land.at[1], False),
        (terms_ref.at[3], parts.at[place, 0], False),
        (terms_ref.at[1], parts.at[place, 1], True),
    ]
    plan, start, receive, sent = handed(
        me, distance, behind, ahead, moves, move_send, move_recv
    )
    start(plan[:2])
    receive(plan[:2])
    start(plan[2:])
    mine = diag_ref[...] - land[0] - land[1]
    out_diag_ref[...] = mine
    diag_full[place] = mine
    spread = Spread(size, place, diag_full, diag_send, diag_recv)
    spread.start_own()
    spread.forward()
    spread.finish()
    part_spread = Spread(size, place, parts, part_send, part_recv)
    blocks = diag_full.shape[0]

    def beside(j):
        @pl.when(j == 1)
        def _():
            receive(plan[2:])
            part_spread.start_own()

        @pl.when(j == blocks - 1)
        def _():
            part_spread.forward()

    factor_kernel(diag_full, high, low, work, beside)
    part_spread.finish()
    sent(plan)
    put_terms(place, high, low, parts, out_ref, solved_high, solved_low)


def step(distance, terms_in, diag_rows):
    times, size = lax.axis_size("tm"), lax.axis_size("swath")
    rows, order = diag_rows.shape
    vmem = pl.BlockSpec(memory_space=pltpu.VMEM)
    dma = pltpu.SemaphoreType.DMA
    return pl.pallas_call(
        functools.partial(step_kernel, distance, times, size),
        out_shape=(
            jax.ShapeDtypeStruct((4, rows, order), jnp.float32),
            jax.ShapeDtypeStruct((rows, order), jnp.float32),
        ),
        in_specs=[vmem] * 2,
        out_specs=(vmem,) * 2,
        scratch_shapes=[
            pltpu.VMEM((2, rows, order), jnp.float32),
            pltpu.VMEM((size, rows, order), jnp.float32),
            pltpu.VMEM((size, 2, rows, order), jnp.float32),
            pltpu.VMEM((order, order), jnp.bfloat16),
            pltpu.VMEM((order, order), jnp.bfloat16),
            pltpu.VMEM((size, rows, order), jnp.float32),
            pltpu.VMEM((order, 2 * order), jnp.bfloat16),
            pltpu.VMEM((order, 2 * order), jnp.bfloat16),
            dma((4,)),
            dma((4,)),
            dma((size - 1,)),
            dma((size - 1,)),
            dma((size - 1,)),
            dma((size - 1,)),
        ],
        compiler_params=pltpu.CompilerParams(collective_id=distance, has_side_effects=True),
    )(terms_in, diag_rows)


def last_kernel(distance, times, size, terms_ref, diag_ref, out_diag_ref, out_coup_ref, land, move_send, move_recv):
    place, me, behind, ahead = greet(distance, times, size, False)
    moves = [
        (terms_ref.at[3], land.at[2], False),
        (terms_ref.at[0], land.at[0], True),
        (terms_ref.at[2], land.at[1], False),
    ]
    plan, start, receive, sent = handed(
        me, distance, behind, ahead, moves, move_send, move_recv
    )
    start(plan)
    receive(plan)
    out_coup_ref[...] = -land[2]
    out_diag_ref[...] = diag_ref[...] - land[0] - land[1]
    sent(plan)


def last(distance, terms_in, diag_rows):
    times, size = lax.axis_size("tm"), lax.axis_size("swath")
    rows, order = diag_rows.shape
    vmem = pl.BlockSpec(memory_space=pltpu.VMEM)
    return pl.pallas_call(
        functools.partial(last_kernel, distance, times, size),
        out_shape=(jax.ShapeDtypeStruct((rows, order), jnp.float32),) * 2,
        in_specs=[vmem] * 2,
        out_specs=(vmem,) * 2,
        scratch_shapes=[
            pltpu.VMEM((3, rows, order), jnp.float32),
            pltpu.SemaphoreType.DMA((3,)),
            pltpu.SemaphoreType.DMA((3,)),
        ],
        compiler_params=pltpu.CompilerParams(collective_id=distance, has_side_effects=True),
    )(terms_in, diag_rows)


def weigh_kernel(total_slots, block_rows, design_ref, process_ref, routes_ref, counts_ref, near_ref, sent_ref):
    me = lax.axis_index("tm")
    block_count = routes_ref.shape[1]
    slot_count = block_count // 2
    weighted = []
    for r in range(block_count):
        raw = design_ref[r * block_rows : (r + 1) * block_rows, :].astype(jnp.float32)
        mean_sq = jnp.mean(raw * raw, axis=-1, keepdims=True)
        weighted.append((raw * lax.rsqrt(4.0 * total_slots * (mean_sq + 1e-06))).astype(jnp.bfloat16))
    for out_ref, owner in ((near_ref, me), (sent_ref, me + 1)):
        place = jnp.int32(0)
        chosen = [jnp.full((), -1, jnp.int32) for _ in range(slot_count)]
        for r in range(block_count):
            named = routes_ref[0, r] == owner
            live = r < counts_ref[0, 0]
            for k in range(slot_count):
                chosen[k] = jnp.where(named & live & (place == k), r, chosen[k])
            place = place + named.astype(jnp.int32)
        for k in range(slot_count):
            block = jnp.zeros(weighted[0].shape, jnp.float32)
            for r in range(block_count):
                block = jnp.where(chosen[k] == r, weighted[r].astype(jnp.float32), block)
            out_ref[k * block_rows : (k + 1) * block_rows, :] = block.astype(jnp.bfloat16)
        out_ref[slot_count * block_rows :, :] = process_ref[...]


def weigh(design, process, routes, counts, total_slots):
    order = process.shape[1]
    block_count = routes.shape[1]
    block_rows = design.shape[0] // block_count
    rows = block_count // 2 * block_rows + process.shape[0]
    vmem, smem = (pl.BlockSpec(memory_space=m) for m in (pltpu.VMEM, pltpu.SMEM))
    return pl.pallas_call(
        functools.partial(weigh_kernel, total_slots, block_rows),
        out_shape=(jax.ShapeDtypeStruct((rows, order), jnp.bfloat16),) * 2,
        in_specs=[vmem, vmem, smem, smem],
        out_specs=(vmem,) * 2,
    )(design, process, routes, counts)


def first_kernel(times, size, near_ref, sent_ref, prior_ref, out_ref, out_diag_ref, near, far, prior,
                 diag_full, parts, high, low, work, solved_high, solved_low, move_send, move_recv,
                 near_send, near_recv, prior_send, prior_recv, far_send, far_recv):
    place, me, behind, ahead = greet(1, times, size, True)
    rows, order = diag_full.shape[1:]
    observed = near.shape[1] - rows
    plan, start, receive, sent = handed(
        me, 1, behind, ahead, [(sent_ref, far.at[place], True)], move_send, move_recv
    )
    start(plan)
    near_spread = Spread(size, place, near, near_send, near_recv, near_ref)
    prior_spread = Spread(size, place, prior, prior_send, prior_recv, prior_ref)
    near_spread.start_own()
    prior_spread.start_own()
    near[place] = near_ref[...]
    prior[place] = prior_ref[...]
    receive(plan)
    far_spread = Spread(size, place, far, far_send, far_recv)
    far_spread.start_own()
    near_spread.forward()
    prior_spread.forward()
    near_spread.finish()
    prior_spread.finish()
    far_spread.forward()
    square = (rows, rows)
    unit = lax.broadcasted_iota(jnp.int32, square, 0) == lax.broadcasted_iota(jnp.int32, square, 1)

    def add_grams(source):
        for b in range(size):
            cut = slice(b * rows, (b + 1) * rows)
            total = source[b, observed:].astype(jnp.float32)
            for i in range(size):
                total = total + lax.dot_general(
                    source[i, :observed, cut],
                    source[i, :observed, :],
                    (((0,), (0,)), ((), ())),
                    preferred_element_type=jnp.float32,
                )
            yield b, cut, total

    for b, cut, total in add_grams(near):
        diag_full[b] = total
        diag_full[b, :, cut] += jnp.where(unit, jnp.broadcast_to(prior[b][:1], square), 0.0)
        parts[b, 0] = near[b, observed:].astype(jnp.float32)
    far_spread.finish()
    for b, cut, total in add_grams(far):
        diag_full[b] += total
        for q in range(size):
            turned = far[q, observed:, cut].astype(jnp.float32).T
            parts[b, 1, :, q * rows : (q + 1) * rows] = turned
    out_diag_ref[...] = diag_full[place]
    factor_kernel(diag_full, high, low, work)
    sent(plan)
    put_terms(place, high, low, parts, out_ref, solved_high, solved_low)


def first(near, sent, prior):
    times, size = lax.axis_size("tm"), lax.axis_size("swath")
    order = near.shape[1]
    rows = order // size
    vmem = pl.BlockSpec(memory_space=pltpu.VMEM)
    dma = pltpu.SemaphoreType.DMA
    return pl.pallas_call(
        functools.partial(first_kernel, times, size),
        out_shape=(
            jax.ShapeDtypeStruct((4, rows, order), jnp.float32),
            jax.ShapeDtypeStruct((rows, order), jnp.float32),
        ),
        in_specs=[vmem] * 3,
        out_specs=(vmem,) * 2,
        scratch_shapes=[
            pltpu.VMEM((size,) + near.shape, jnp.bfloat16),
            pltpu.VMEM((size,) + near.shape, jnp.bfloat16),
            pltpu.VMEM((size,) + prior.shape, jnp.float32),
            pltpu.VMEM((size, rows, order), jnp.float32),
            pltpu.VMEM((size, 2, rows, order), jnp.float32),
            pltpu.VMEM((order, order), jnp.bfloat16),
            pltpu.VMEM((order, order), jnp.bfloat16),
            pltpu.VMEM((size, rows, order), jnp.float32),
            pltpu.VMEM((order, 2 * order), jnp.bfloat16),
            pltpu.VMEM((order, 2 * order), jnp.bfloat16),
            dma((1,)),
            dma((1,)),
        ]
        + [dma((size - 1,))] * 6,
        compiler_params=pltpu.CompilerParams(collective_id=0, has_side_effects=True),
    )(near, sent, prior)


def shards(design, process, prior_prec, routes, counts):
    row_count = process.shape[1]
    block_count = routes.shape[1]
    block_rows = design.shape[1] // block_count
    total_slots = 2 * (block_count // 2) * block_rows * lax.axis_size("swath")
    near, sent = weigh(design[0], process[0], routes, counts, total_slots)
    prior = jnp.broadcast_to(prior_prec, (8, row_count))
    out, diag_rows = first(near, sent, prior)
    for level in range(1, LEVELS):
        out, diag_rows = step(2 ** (level - 1), out, diag_rows)
    diag_rows, coup_rows = last(2 ** (LEVELS - 1), out, diag_rows)
    return (diag_rows[None], coup_rows[None])


def solution(mesh):
    return jax.shard_map(
        shards,
        mesh=mesh,
        in_specs=(
            P("tm", "swath", None),
            P("tm", "swath", None),
            P("tm", "swath"),
            P("tm", "swath"),
            P("tm", "swath"),
        ),
        out_specs=(P("tm", "swath", None), P("tm", "swath", None)),
        check_vma=False,
    )
```

```python
import functools

import jax
import jax.numpy as jnp
from jax import lax
from jax.experimental import pallas as pl
from jax.experimental.pallas import tpu as pltpu
from jax.sharding import PartitionSpec as P

LEVELS = 3
PIECES = 2


def split(x):
    high = x.astype(jnp.bfloat16)
    return high, (x - high.astype(jnp.float32)).astype(jnp.bfloat16)


def dot3(a, b, left):
    (ah, al), (bh, bl) = a, b
    dot = functools.partial(
        lax.dot_general,
        dimension_numbers=(((left,), (0,)), ((), ())),
        preferred_element_type=jnp.float32,
    )
    return dot(ah, bh) + (dot(ah, bl) + dot(al, bh))


def factor_inverse(m, width=8):
    n = m.shape[0]
    groups = n // width
    rows = [m[width * g : width * (g + 1), :] for g in range(groups)]
    lane = lax.broadcasted_iota(jnp.int32, (width, n), 1)
    sub = lax.broadcasted_iota(jnp.int32, (width, n), 0)
    spread = lambda x: jnp.broadcast_to(x, (width, n))
    for g in range(groups):
        first = width * g
        inside = (lane >= first) & (lane < first + width)
        columns = {
            h: [spread(rows[h][:, first + s : first + s + 1]) for s in range(width)]
            for h in range(g, groups)
        }
        entry = {
            (k, s): spread(columns[g][s][k : k + 1, :])
            for s in range(width)
            for k in range(s, width)
        }
        solved = [
            jnp.where(lane == first + s, 1.0, jnp.where(inside, 0.0, spread(rows[g][s : s + 1, :])))
            for s in range(width)
        ]
        scale, lower = [], {}
        for s in range(width):
            scale.append(lax.rsqrt(entry[s, s]))
            solved[s] = solved[s] * scale[s]
            for k in range(s + 1, width):
                lower[k, s] = entry[k, s] * scale[s]
            for k in range(s + 1, width):
                for t in range(s + 1, k + 1):
                    entry[k, t] = entry[k, t] - lower[k, s] * lower[t, s]
                solved[k] = solved[k] - lower[k, s] * solved[s]
        back = list(solved)
        for s in range(width - 1, -1, -1):
            back[s] = back[s] * scale[s]
            for k in range(s):
                back[k] = back[k] - lower[s, k] * back[s]
        for h in range(g + 1, groups):
            left = jnp.where(inside, 0.0, rows[h])
            for s in range(width - 1, -1, -1):
                left = left - columns[h][s] * back[s]
            rows[h] = left
        group = solved[0]
        for s in range(1, width):
            group = jnp.where(sub == s, solved[s], group)
        rows[g] = group
    out = jnp.concatenate(rows, axis=0)
    down = lax.broadcasted_iota(jnp.int32, (n, n), 0)
    across = lax.broadcasted_iota(jnp.int32, (n, n), 1)
    return jnp.where(down >= across, out, 0.0)


def factor_kernel(diag_ref, high, low, work, beside=None):
    blocks, rows, order = diag_ref.shape
    work[...] = diag_ref[...]
    for i in range(blocks):
        for k in range(i, blocks):
            here = work[i, :, k * rows : (k + 1) * rows]
            there = work[k, :, i * rows : (i + 1) * rows]
            work[i, :, k * rows : (k + 1) * rows] = 0.5 * (here + there.T)
    down = lax.broadcasted_iota(jnp.int32, (rows, rows), 0)
    across = lax.broadcasted_iota(jnp.int32, (rows, rows), 1)
    unit = jnp.where(down == across, 1.0, 0.0)
    column_block = lax.broadcasted_iota(jnp.int32, (rows, order), 1) // rows

    def step(j, carry):
        at = pl.ds(pl.multiple_of(j * rows, rows), rows)
        if beside is not None:
            beside(j)
        inverse = factor_inverse(work[j, :, at])
        work[j, :, at] = unit
        solved = dot3(split(inverse), split(work[j]), 1)
        solved_high, solved_low = split(solved)
        high[at, :] = solved_high
        low[at, :] = solved_low
        for i in range(1, blocks):

            @pl.when(i > j)
            def _():
                cut = slice(i * rows, (i + 1) * rows)
                left = (high[at, cut], low[at, cut])
                work[i, :, at] = jnp.zeros((rows, rows), jnp.float32)
                work[i] = work[i] - dot3(left, (solved_high, solved_low), 0)

        keep = column_block <= j
        high[at, :] = jnp.where(keep, solved_high, 0.0).astype(jnp.bfloat16)
        low[at, :] = jnp.where(keep, solved_low, 0.0).astype(jnp.bfloat16)
        return carry

    lax.fori_loop(0, blocks, step, 0)


def put_terms(index, inverse_high, inverse_low, parts_ref, out_ref, high, low):
    blocks, _, rows, order = parts_ref.shape
    for part in range(2):
        across = slice(part * order, (part + 1) * order)
        right = [split(parts_ref[i, part]) for i in range(blocks)]
        right = [jnp.concatenate([r[k] for r in right], axis=0) for k in range(2)]
        for j in range(blocks):
            at, deep = slice(j * rows, (j + 1) * rows), (j + 1) * rows
            left = (inverse_high[at, :deep], inverse_low[at, :deep])
            solved = dot3(left, (right[0][:deep], right[1][:deep]), 1)
            solved_high, solved_low = split(solved)
            high[at, across] = solved_high
            low[at, across] = solved_low
    mine = index * rows
    for k, (first, second) in enumerate(((0, 0), (0, 1), (1, 1), (1, 0))):
        cut = pl.ds(pl.multiple_of(first * order + mine, rows), rows)
        across = slice(second * order, (second + 1) * order)
        out_ref[k] = dot3((high[:, cut], low[:, cut]), (high[:, across], low[:, across]), 0)


MESH = pl.DeviceIdType.MESH


def across(place, bit):
    return place + bit - 2 * bit * ((place // bit) % 2)


class Spread:
    def __init__(self, size, place, block, send_sem, recv_sem, own=None, cut=None, base=0):
        bits = [size >> (k + 1) for k in range(size.bit_length() - 1)]
        self.plan = [(b, 0) for b in bits]
        for k, b in enumerate(bits):
            earlier = [0]
            for e in bits[:k]:
                earlier += [m + e for m in earlier]
            self.plan += [(b, m) for m in earlier if m]
        self.copies, self.arrived = [], set()
        part = lambda held: block.at[held] if cut is None else block.at[held, cut]
        for k, (b, m) in enumerate(self.plan):
            held = place
            for e in bits:
                if m & e:
                    held = across(held, e)
            self.copies.append(
                pltpu.make_async_remote_copy(
                    src_ref=own if own is not None and m == 0 else part(held),
                    dst_ref=part(held),
                    send_sem=send_sem.at[base + k],
                    recv_sem=recv_sem.at[base + k],
                    device_id={"swath": across(place, b)},
                    device_id_type=MESH,
                )
            )

    def start_own(self):
        for copy, (b, m) in zip(self.copies, self.plan):
            if m == 0:
                copy.start()

    def forward(self):
        for copy, (b, m) in zip(self.copies, self.plan):
            if m:
                last = m & -m
                source = self.plan.index((last, m - last))
                if source not in self.arrived:
                    self.copies[source].wait_recv()
                    self.arrived.add(source)
                copy.start()

    def finish(self):
        for k, copy in enumerate(self.copies):
            if k not in self.arrived:
                copy.wait_recv()
        for copy in self.copies:
            copy.wait_send()


def greet(distance, times, size, spread_too):
    place, me = lax.axis_index("swath"), lax.axis_index("tm")
    barrier = pltpu.get_barrier_semaphore()
    behind, ahead = me >= distance, me + distance < times

    @pl.when(behind)
    def _():
        pl.semaphore_signal(barrier, inc=1, device_id={"tm": me - distance}, device_id_type=MESH)

    @pl.when(ahead)
    def _():
        pl.semaphore_signal(barrier, inc=1, device_id={"tm": me + distance}, device_id_type=MESH)

    count = behind.astype(jnp.int32) + ahead.astype(jnp.int32)
    if spread_too:
        bits = [size >> (k + 1) for k in range(size.bit_length() - 1)]
        for b in bits:
            pl.semaphore_signal(
                barrier, inc=1, device_id={"swath": across(place, b)}, device_id_type=MESH
            )
        count = count + len(bits)
    pl.semaphore_wait(barrier, count)
    return place, me, behind, ahead


def handed(me, distance, behind, ahead, moves, send_sem, recv_sem):
    plan = []
    for k, (source, target, up) in enumerate(moves):
        copy = pltpu.make_async_remote_copy(
            src_ref=source,
            dst_ref=target,
            send_sem=send_sem.at[k],
            recv_sem=recv_sem.at[k],
            device_id={"tm": me + distance if up else me - distance},
            device_id_type=MESH,
        )
        plan.append((copy, target, ahead if up else behind, behind if up else ahead))

    def start(items):
        for copy, target, sends, receives in items:
            pl.when(sends)(copy.start)

    def receive(items):
        for copy, target, sends, receives in items:
            pl.when(receives)(copy.wait_recv)

            @pl.when(jnp.logical_not(receives))
            def _():
                target[...] = jnp.zeros(target.shape, target.dtype)

    def sent(items):
        for copy, target, sends, receives in items:
            pl.when(sends)(copy.wait_send)

    return plan, start, receive, sent


def step_kernel(distance, times, size, terms_ref, diag_ref, out_ref, out_diag_ref, land, diag_full,
                parts, high, low, work, solved_high, solved_low, move_send, move_recv,
                diag_send, diag_recv, part_send, part_recv):
    place, me, behind, ahead = greet(distance, times, size, True)
    piece = diag_ref.shape[0] // PIECES
    cuts = [pl.ds(c * piece, piece) for c in range(PIECES)]
    moves = []
    for cut in cuts:
        moves.append((terms_ref.at[0, cut], land.at[0, cut], True))
        moves.append((terms_ref.at[2, cut], land.at[1, cut], False))
    moves.append((terms_ref.at[3], parts.at[place, 0], False))
    moves.append((terms_ref.at[1], parts.at[place, 1], True))
    plan, start, receive, sent = handed(
        me, distance, behind, ahead, moves, move_send, move_recv
    )
    coupled = 2 * PIECES
    start(plan[:coupled])
    spreads = []
    for c, cut in enumerate(cuts):
        receive(plan[2 * c : 2 * c + 2])
        if c == PIECES - 1:
            start(plan[coupled:])
        mine = diag_ref[cut] - land[0, cut] - land[1, cut]
        out_diag_ref[cut] = mine
        diag_full[place, cut] = mine
        spreads.append(
            Spread(size, place, diag_full, diag_send, diag_recv, None, cut, c * (size - 1))
        )
        spreads[c].start_own()
    for spread in spreads:
        spread.forward()
    for spread in spreads:
        spread.finish()
    part_spread = Spread(size, place, parts, part_send, part_recv)
    blocks = diag_full.shape[0]

    def beside(j):
        @pl.when(j == 1)
        def _():
            receive(plan[coupled:])
            part_spread.start_own()

        @pl.when(j == blocks - 1)
        def _():
            part_spread.forward()

    factor_kernel(diag_full, high, low, work, beside)
    part_spread.finish()
    sent(plan)
    put_terms(place, high, low, parts, out_ref, solved_high, solved_low)


def step(distance, terms_in, diag_rows):
    times, size = lax.axis_size("tm"), lax.axis_size("swath")
    rows, order = diag_rows.shape
    vmem = pl.BlockSpec(memory_space=pltpu.VMEM)
    dma = pltpu.SemaphoreType.DMA
    return pl.pallas_call(
        functools.partial(step_kernel, distance, times, size),
        out_shape=(
            jax.ShapeDtypeStruct((4, rows, order), jnp.float32),
            jax.ShapeDtypeStruct((rows, order), jnp.float32),
        ),
        in_specs=[vmem] * 2,
        out_specs=(vmem,) * 2,
        scratch_shapes=[
            pltpu.VMEM((2, rows, order), jnp.float32),
            pltpu.VMEM((size, rows, order), jnp.float32),
            pltpu.VMEM((size, 2, rows, order), jnp.float32),
            pltpu.VMEM((order, order), jnp.bfloat16),
            pltpu.VMEM((order, order), jnp.bfloat16),
            pltpu.VMEM((size, rows, order), jnp.float32),
            pltpu.VMEM((order, 2 * order), jnp.bfloat16),
            pltpu.VMEM((order, 2 * order), jnp.bfloat16),
            dma((2 * PIECES + 2,)),
            dma((2 * PIECES + 2,)),
            dma((PIECES * (size - 1),)),
            dma((PIECES * (size - 1),)),
            dma((size - 1,)),
            dma((size - 1,)),
        ],
        compiler_params=pltpu.CompilerParams(collective_id=distance, has_side_effects=True),
    )(terms_in, diag_rows)


def last_kernel(distance, times, size, terms_ref, diag_ref, out_diag_ref, out_coup_ref, land, move_send, move_recv):
    place, me, behind, ahead = greet(distance, times, size, False)
    moves = [
        (terms_ref.at[3], land.at[2], False),
        (terms_ref.at[0], land.at[0], True),
        (terms_ref.at[2], land.at[1], False),
    ]
    plan, start, receive, sent = handed(
        me, distance, behind, ahead, moves, move_send, move_recv
    )
    start(plan)
    receive(plan)
    out_coup_ref[...] = -land[2]
    out_diag_ref[...] = diag_ref[...] - land[0] - land[1]
    sent(plan)


def last(distance, terms_in, diag_rows):
    times, size = lax.axis_size("tm"), lax.axis_size("swath")
    rows, order = diag_rows.shape
    vmem = pl.BlockSpec(memory_space=pltpu.VMEM)
    return pl.pallas_call(
        functools.partial(last_kernel, distance, times, size),
        out_shape=(jax.ShapeDtypeStruct((rows, order), jnp.float32),) * 2,
        in_specs=[vmem] * 2,
        out_specs=(vmem,) * 2,
        scratch_shapes=[
            pltpu.VMEM((3, rows, order), jnp.float32),
            pltpu.SemaphoreType.DMA((3,)),
            pltpu.SemaphoreType.DMA((3,)),
        ],
        compiler_params=pltpu.CompilerParams(collective_id=distance, has_side_effects=True),
    )(terms_in, diag_rows)


def weigh_kernel(total_slots, block_rows, design_ref, process_ref, routes_ref, counts_ref, near_ref, sent_ref):
    me = lax.axis_index("tm")
    block_count = routes_ref.shape[1]
    slot_count = block_count // 2
    weighted = []
    for r in range(block_count):
        raw = design_ref[r * block_rows : (r + 1) * block_rows, :].astype(jnp.float32)
        mean_sq = jnp.mean(raw * raw, axis=-1, keepdims=True)
        weighted.append((raw * lax.rsqrt(4.0 * total_slots * (mean_sq + 1e-06))).astype(jnp.bfloat16))
    for out_ref, owner in ((near_ref, me), (sent_ref, me + 1)):
        place = jnp.int32(0)
        chosen = [jnp.full((), -1, jnp.int32) for _ in range(slot_count)]
        for r in range(block_count):
            named = routes_ref[0, r] == owner
            live = r < counts_ref[0, 0]
            for k in range(slot_count):
                chosen[k] = jnp.where(named & live & (place == k), r, chosen[k])
            place = place + named.astype(jnp.int32)
        for k in range(slot_count):
            block = jnp.zeros(weighted[0].shape, jnp.float32)
            for r in range(block_count):
                block = jnp.where(chosen[k] == r, weighted[r].astype(jnp.float32), block)
            out_ref[k * block_rows : (k + 1) * block_rows, :] = block.astype(jnp.bfloat16)
        out_ref[slot_count * block_rows :, :] = process_ref[...]


def weigh(design, process, routes, counts, total_slots):
    order = process.shape[1]
    block_count = routes.shape[1]
    block_rows = design.shape[0] // block_count
    rows = block_count // 2 * block_rows + process.shape[0]
    vmem, smem = (pl.BlockSpec(memory_space=m) for m in (pltpu.VMEM, pltpu.SMEM))
    return pl.pallas_call(
        functools.partial(weigh_kernel, total_slots, block_rows),
        out_shape=(jax.ShapeDtypeStruct((rows, order), jnp.bfloat16),) * 2,
        in_specs=[vmem, vmem, smem, smem],
        out_specs=(vmem,) * 2,
    )(design, process, routes, counts)


def first_kernel(times, size, near_ref, sent_ref, prior_ref, out_ref, out_diag_ref, near, far, prior,
                 diag_full, parts, high, low, work, solved_high, solved_low, move_send, move_recv,
                 near_send, near_recv, prior_send, prior_recv, far_send, far_recv):
    place, me, behind, ahead = greet(1, times, size, True)
    rows, order = diag_full.shape[1:]
    observed = near.shape[1] - rows
    plan, start, receive, sent = handed(
        me, 1, behind, ahead, [(sent_ref, far.at[place], True)], move_send, move_recv
    )
    start(plan)
    near_spread = Spread(size, place, near, near_send, near_recv, near_ref)
    prior_spread = Spread(size, place, prior, prior_send, prior_recv, prior_ref)
    near_spread.start_own()
    prior_spread.start_own()
    near[place] = near_ref[...]
    prior[place] = prior_ref[...]
    receive(plan)
    far_spread = Spread(size, place, far, far_send, far_recv)
    far_spread.start_own()
    near_spread.forward()
    prior_spread.forward()
    near_spread.finish()
    prior_spread.finish()
    far_spread.forward()
    square = (rows, rows)
    unit = lax.broadcasted_iota(jnp.int32, square, 0) == lax.broadcasted_iota(jnp.int32, square, 1)

    def add_grams(source):
        for b in range(size):
            cut = slice(b * rows, (b + 1) * rows)
            total = source[b, observed:].astype(jnp.float32)
            for i in range(size):
                total = total + lax.dot_general(
                    source[i, :observed, cut],
                    source[i, :observed, :],
                    (((0,), (0,)), ((), ())),
                    preferred_element_type=jnp.float32,
                )
            yield b, cut, total

    for b, cut, total in add_grams(near):
        diag_full[b] = total
        diag_full[b, :, cut] += jnp.where(unit, jnp.broadcast_to(prior[b][:1], square), 0.0)
        parts[b, 0] = near[b, observed:].astype(jnp.float32)
    far_spread.finish()
    for b, cut, total in add_grams(far):
        diag_full[b] += total
        for q in range(size):
            turned = far[q, observed:, cut].astype(jnp.float32).T
            parts[b, 1, :, q * rows : (q + 1) * rows] = turned
    out_diag_ref[...] = diag_full[place]
    factor_kernel(diag_full, high, low, work)
    sent(plan)
    put_terms(place, high, low, parts, out_ref, solved_high, solved_low)


def first(near, sent, prior):
    times, size = lax.axis_size("tm"), lax.axis_size("swath")
    order = near.shape[1]
    rows = order // size
    vmem = pl.BlockSpec(memory_space=pltpu.VMEM)
    dma = pltpu.SemaphoreType.DMA
    return pl.pallas_call(
        functools.partial(first_kernel, times, size),
        out_shape=(
            jax.ShapeDtypeStruct((4, rows, order), jnp.float32),
            jax.ShapeDtypeStruct((rows, order), jnp.float32),
        ),
        in_specs=[vmem] * 3,
        out_specs=(vmem,) * 2,
        scratch_shapes=[
            pltpu.VMEM((size,) + near.shape, jnp.bfloat16),
            pltpu.VMEM((size,) + near.shape, jnp.bfloat16),
            pltpu.VMEM((size,) + prior.shape, jnp.float32),
            pltpu.VMEM((size, rows, order), jnp.float32),
            pltpu.VMEM((size, 2, rows, order), jnp.float32),
            pltpu.VMEM((order, order), jnp.bfloat16),
            pltpu.VMEM((order, order), jnp.bfloat16),
            pltpu.VMEM((size, rows, order), jnp.float32),
            pltpu.VMEM((order, 2 * order), jnp.bfloat16),
            pltpu.VMEM((order, 2 * order), jnp.bfloat16),
            dma((1,)),
            dma((1,)),
        ]
        + [dma((size - 1,))] * 6,
        compiler_params=pltpu.CompilerParams(collective_id=0, has_side_effects=True),
    )(near, sent, prior)


def shards(design, process, prior_prec, routes, counts):
    row_count = process.shape[1]
    block_count = routes.shape[1]
    block_rows = design.shape[1] // block_count
    total_slots = 2 * (block_count // 2) * block_rows * lax.axis_size("swath")
    near, sent = weigh(design[0], process[0], routes, counts, total_slots)
    prior = jnp.broadcast_to(prior_prec, (8, row_count))
    out, diag_rows = first(near, sent, prior)
    for level in range(1, LEVELS):
        out, diag_rows = step(2 ** (level - 1), out, diag_rows)
    diag_rows, coup_rows = last(2 ** (LEVELS - 1), out, diag_rows)
    return (diag_rows[None], coup_rows[None])


def solution(mesh):
    return jax.shard_map(
        shards,
        mesh=mesh,
        in_specs=(
            P("tm", "swath", None),
            P("tm", "swath", None),
            P("tm", "swath"),
            P("tm", "swath"),
            P("tm", "swath"),
        ),
        out_specs=(P("tm", "swath", None), P("tm", "swath", None)),
        check_vma=False,
    )
```

```python
import functools

import jax
import jax.numpy as jnp
from jax import lax
from jax.experimental import pallas as pl
from jax.experimental.pallas import tpu as pltpu
from jax.sharding import PartitionSpec as P

LEVELS = 3
PIECES = 4


def split(x):
    high = x.astype(jnp.bfloat16)
    return high, (x - high.astype(jnp.float32)).astype(jnp.bfloat16)


def dot3(a, b, left):
    (ah, al), (bh, bl) = a, b
    dot = functools.partial(
        lax.dot_general,
        dimension_numbers=(((left,), (0,)), ((), ())),
        preferred_element_type=jnp.float32,
    )
    return dot(ah, bh) + (dot(ah, bl) + dot(al, bh))


def factor_inverse(m, width=8):
    n = m.shape[0]
    groups = n // width
    rows = [m[width * g : width * (g + 1), :] for g in range(groups)]
    lane = lax.broadcasted_iota(jnp.int32, (width, n), 1)
    sub = lax.broadcasted_iota(jnp.int32, (width, n), 0)
    spread = lambda x: jnp.broadcast_to(x, (width, n))
    for g in range(groups):
        first = width * g
        inside = (lane >= first) & (lane < first + width)
        columns = {
            h: [spread(rows[h][:, first + s : first + s + 1]) for s in range(width)]
            for h in range(g, groups)
        }
        entry = {
            (k, s): spread(columns[g][s][k : k + 1, :])
            for s in range(width)
            for k in range(s, width)
        }
        solved = [
            jnp.where(lane == first + s, 1.0, jnp.where(inside, 0.0, spread(rows[g][s : s + 1, :])))
            for s in range(width)
        ]
        scale, lower = [], {}
        for s in range(width):
            scale.append(lax.rsqrt(entry[s, s]))
            solved[s] = solved[s] * scale[s]
            for k in range(s + 1, width):
                lower[k, s] = entry[k, s] * scale[s]
            for k in range(s + 1, width):
                for t in range(s + 1, k + 1):
                    entry[k, t] = entry[k, t] - lower[k, s] * lower[t, s]
                solved[k] = solved[k] - lower[k, s] * solved[s]
        back = list(solved)
        for s in range(width - 1, -1, -1):
            back[s] = back[s] * scale[s]
            for k in range(s):
                back[k] = back[k] - lower[s, k] * back[s]
        for h in range(g + 1, groups):
            left = jnp.where(inside, 0.0, rows[h])
            for s in range(width - 1, -1, -1):
                left = left - columns[h][s] * back[s]
            rows[h] = left
        group = solved[0]
        for s in range(1, width):
            group = jnp.where(sub == s, solved[s], group)
        rows[g] = group
    out = jnp.concatenate(rows, axis=0)
    down = lax.broadcasted_iota(jnp.int32, (n, n), 0)
    across = lax.broadcasted_iota(jnp.int32, (n, n), 1)
    return jnp.where(down >= across, out, 0.0)


def factor_kernel(diag_ref, high, low, work, beside=None):
    blocks, rows, order = diag_ref.shape
    work[...] = diag_ref[...]
    for i in range(blocks):
        for k in range(i, blocks):
            here = work[i, :, k * rows : (k + 1) * rows]
            there = work[k, :, i * rows : (i + 1) * rows]
            work[i, :, k * rows : (k + 1) * rows] = 0.5 * (here + there.T)
    down = lax.broadcasted_iota(jnp.int32, (rows, rows), 0)
    across = lax.broadcasted_iota(jnp.int32, (rows, rows), 1)
    unit = jnp.where(down == across, 1.0, 0.0)
    column_block = lax.broadcasted_iota(jnp.int32, (rows, order), 1) // rows

    def step(j, carry):
        at = pl.ds(pl.multiple_of(j * rows, rows), rows)
        if beside is not None:
            beside(j)
        inverse = factor_inverse(work[j, :, at])
        work[j, :, at] = unit
        solved = dot3(split(inverse), split(work[j]), 1)
        solved_high, solved_low = split(solved)
        high[at, :] = solved_high
        low[at, :] = solved_low
        for i in range(1, blocks):

            @pl.when(i > j)
            def _():
                cut = slice(i * rows, (i + 1) * rows)
                left = (high[at, cut], low[at, cut])
                work[i, :, at] = jnp.zeros((rows, rows), jnp.float32)
                work[i] = work[i] - dot3(left, (solved_high, solved_low), 0)

        keep = column_block <= j
        high[at, :] = jnp.where(keep, solved_high, 0.0).astype(jnp.bfloat16)
        low[at, :] = jnp.where(keep, solved_low, 0.0).astype(jnp.bfloat16)
        return carry

    lax.fori_loop(0, blocks, step, 0)


def put_terms(index, inverse_high, inverse_low, parts_ref, out_ref, high, low):
    blocks, _, rows, order = parts_ref.shape
    for part in range(2):
        across = slice(part * order, (part + 1) * order)
        right = [split(parts_ref[i, part]) for i in range(blocks)]
        right = [jnp.concatenate([r[k] for r in right], axis=0) for k in range(2)]
        for j in range(blocks):
            at, deep = slice(j * rows, (j + 1) * rows), (j + 1) * rows
            left = (inverse_high[at, :deep], inverse_low[at, :deep])
            solved = dot3(left, (right[0][:deep], right[1][:deep]), 1)
            solved_high, solved_low = split(solved)
            high[at, across] = solved_high
            low[at, across] = solved_low
    mine = index * rows
    for k, (first, second) in enumerate(((0, 0), (0, 1), (1, 1), (1, 0))):
        cut = pl.ds(pl.multiple_of(first * order + mine, rows), rows)
        across = slice(second * order, (second + 1) * order)
        out_ref[k] = dot3((high[:, cut], low[:, cut]), (high[:, across], low[:, across]), 0)


MESH = pl.DeviceIdType.MESH


def across(place, bit):
    return place + bit - 2 * bit * ((place // bit) % 2)


class Spread:
    def __init__(self, size, place, block, send_sem, recv_sem, own=None, cut=None, base=0):
        bits = [size >> (k + 1) for k in range(size.bit_length() - 1)]
        self.plan = [(b, 0) for b in bits]
        for k, b in enumerate(bits):
            earlier = [0]
            for e in bits[:k]:
                earlier += [m + e for m in earlier]
            self.plan += [(b, m) for m in earlier if m]
        self.copies, self.arrived = [], set()
        part = lambda held: block.at[held] if cut is None else block.at[held, cut]
        for k, (b, m) in enumerate(self.plan):
            held = place
            for e in bits:
                if m & e:
                    held = across(held, e)
            self.copies.append(
                pltpu.make_async_remote_copy(
                    src_ref=own if own is not None and m == 0 else part(held),
                    dst_ref=part(held),
                    send_sem=send_sem.at[base + k],
                    recv_sem=recv_sem.at[base + k],
                    device_id={"swath": across(place, b)},
                    device_id_type=MESH,
                )
            )

    def start_own(self):
        for copy, (b, m) in zip(self.copies, self.plan):
            if m == 0:
                copy.start()

    def forward(self):
        for copy, (b, m) in zip(self.copies, self.plan):
            if m:
                last = m & -m
                source = self.plan.index((last, m - last))
                if source not in self.arrived:
                    self.copies[source].wait_recv()
                    self.arrived.add(source)
                copy.start()

    def finish(self):
        for k, copy in enumerate(self.copies):
            if k not in self.arrived:
                copy.wait_recv()
        for copy in self.copies:
            copy.wait_send()


def greet(distance, times, size, spread_too):
    place, me = lax.axis_index("swath"), lax.axis_index("tm")
    barrier = pltpu.get_barrier_semaphore()
    behind, ahead = me >= distance, me + distance < times

    @pl.when(behind)
    def _():
        pl.semaphore_signal(barrier, inc=1, device_id={"tm": me - distance}, device_id_type=MESH)

    @pl.when(ahead)
    def _():
        pl.semaphore_signal(barrier, inc=1, device_id={"tm": me + distance}, device_id_type=MESH)

    count = behind.astype(jnp.int32) + ahead.astype(jnp.int32)
    if spread_too:
        bits = [size >> (k + 1) for k in range(size.bit_length() - 1)]
        for b in bits:
            pl.semaphore_signal(
                barrier, inc=1, device_id={"swath": across(place, b)}, device_id_type=MESH
            )
        count = count + len(bits)
    pl.semaphore_wait(barrier, count)
    return place, me, behind, ahead


def handed(me, distance, behind, ahead, moves, send_sem, recv_sem):
    plan = []
    for k, (source, target, up) in enumerate(moves):
        copy = pltpu.make_async_remote_copy(
            src_ref=source,
            dst_ref=target,
            send_sem=send_sem.at[k],
            recv_sem=recv_sem.at[k],
            device_id={"tm": me + distance if up else me - distance},
            device_id_type=MESH,
        )
        plan.append((copy, target, ahead if up else behind, behind if up else ahead))

    def start(items):
        for copy, target, sends, receives in items:
            pl.when(sends)(copy.start)

    def receive(items):
        for copy, target, sends, receives in items:
            pl.when(receives)(copy.wait_recv)

            @pl.when(jnp.logical_not(receives))
            def _():
                target[...] = jnp.zeros(target.shape, target.dtype)

    def sent(items):
        for copy, target, sends, receives in items:
            pl.when(sends)(copy.wait_send)

    return plan, start, receive, sent


def step_kernel(distance, times, size, terms_ref, diag_ref, out_ref, out_diag_ref, land, diag_full,
                parts, high, low, work, solved_high, solved_low, move_send, move_recv,
                diag_send, diag_recv, part_send, part_recv):
    place, me, behind, ahead = greet(distance, times, size, True)
    piece = diag_ref.shape[0] // PIECES
    cuts = [pl.ds(c * piece, piece) for c in range(PIECES)]
    moves = []
    for cut in cuts:
        moves.append((terms_ref.at[0, cut], land.at[0, cut], True))
        moves.append((terms_ref.at[2, cut], land.at[1, cut], False))
    moves.append((terms_ref.at[3], parts.at[place, 0], False))
    moves.append((terms_ref.at[1], parts.at[place, 1], True))
    plan, start, receive, sent = handed(
        me, distance, behind, ahead, moves, move_send, move_recv
    )
    coupled = 2 * PIECES
    start(plan[:coupled])
    spreads = []
    for c, cut in enumerate(cuts):
        receive(plan[2 * c : 2 * c + 2])
        if c == PIECES - 1:
            start(plan[coupled:])
        mine = diag_ref[cut] - land[0, cut] - land[1, cut]
        out_diag_ref[cut] = mine
        diag_full[place, cut] = mine
        spreads.append(
            Spread(size, place, diag_full, diag_send, diag_recv, None, cut, c * (size - 1))
        )
        spreads[c].start_own()
    for spread in spreads:
        spread.forward()
    for spread in spreads:
        spread.finish()
    part_spread = Spread(size, place, parts, part_send, part_recv)
    blocks = diag_full.shape[0]

    def beside(j):
        @pl.when(j == 1)
        def _():
            receive(plan[coupled:])
            part_spread.start_own()

        @pl.when(j == blocks - 1)
        def _():
            part_spread.forward()

    factor_kernel(diag_full, high, low, work, beside)
    part_spread.finish()
    sent(plan)
    put_terms(place, high, low, parts, out_ref, solved_high, solved_low)


def step(distance, terms_in, diag_rows):
    times, size = lax.axis_size("tm"), lax.axis_size("swath")
    rows, order = diag_rows.shape
    vmem = pl.BlockSpec(memory_space=pltpu.VMEM)
    dma = pltpu.SemaphoreType.DMA
    return pl.pallas_call(
        functools.partial(step_kernel, distance, times, size),
        out_shape=(
            jax.ShapeDtypeStruct((4, rows, order), jnp.float32),
            jax.ShapeDtypeStruct((rows, order), jnp.float32),
        ),
        in_specs=[vmem] * 2,
        out_specs=(vmem,) * 2,
        scratch_shapes=[
            pltpu.VMEM((2, rows, order), jnp.float32),
            pltpu.VMEM((size, rows, order), jnp.float32),
            pltpu.VMEM((size, 2, rows, order), jnp.float32),
            pltpu.VMEM((order, order), jnp.bfloat16),
            pltpu.VMEM((order, order), jnp.bfloat16),
            pltpu.VMEM((size, rows, order), jnp.float32),
            pltpu.VMEM((order, 2 * order), jnp.bfloat16),
            pltpu.VMEM((order, 2 * order), jnp.bfloat16),
            dma((2 * PIECES + 2,)),
            dma((2 * PIECES + 2,)),
            dma((PIECES * (size - 1),)),
            dma((PIECES * (size - 1),)),
            dma((size - 1,)),
            dma((size - 1,)),
        ],
        compiler_params=pltpu.CompilerParams(collective_id=distance, has_side_effects=True),
    )(terms_in, diag_rows)


def last_kernel(distance, times, size, terms_ref, diag_ref, out_diag_ref, out_coup_ref, land, move_send, move_recv):
    place, me, behind, ahead = greet(distance, times, size, False)
    moves = [
        (terms_ref.at[3], land.at[2], False),
        (terms_ref.at[0], land.at[0], True),
        (terms_ref.at[2], land.at[1], False),
    ]
    plan, start, receive, sent = handed(
        me, distance, behind, ahead, moves, move_send, move_recv
    )
    start(plan)
    receive(plan)
    out_coup_ref[...] = -land[2]
    out_diag_ref[...] = diag_ref[...] - land[0] - land[1]
    sent(plan)


def last(distance, terms_in, diag_rows):
    times, size = lax.axis_size("tm"), lax.axis_size("swath")
    rows, order = diag_rows.shape
    vmem = pl.BlockSpec(memory_space=pltpu.VMEM)
    return pl.pallas_call(
        functools.partial(last_kernel, distance, times, size),
        out_shape=(jax.ShapeDtypeStruct((rows, order), jnp.float32),) * 2,
        in_specs=[vmem] * 2,
        out_specs=(vmem,) * 2,
        scratch_shapes=[
            pltpu.VMEM((3, rows, order), jnp.float32),
            pltpu.SemaphoreType.DMA((3,)),
            pltpu.SemaphoreType.DMA((3,)),
        ],
        compiler_params=pltpu.CompilerParams(collective_id=distance, has_side_effects=True),
    )(terms_in, diag_rows)


def weigh_kernel(total_slots, block_rows, design_ref, process_ref, routes_ref, counts_ref, near_ref, sent_ref):
    me = lax.axis_index("tm")
    block_count = routes_ref.shape[1]
    slot_count = block_count // 2
    weighted = []
    for r in range(block_count):
        raw = design_ref[r * block_rows : (r + 1) * block_rows, :].astype(jnp.float32)
        mean_sq = jnp.mean(raw * raw, axis=-1, keepdims=True)
        weighted.append((raw * lax.rsqrt(4.0 * total_slots * (mean_sq + 1e-06))).astype(jnp.bfloat16))
    for out_ref, owner in ((near_ref, me), (sent_ref, me + 1)):
        place = jnp.int32(0)
        chosen = [jnp.full((), -1, jnp.int32) for _ in range(slot_count)]
        for r in range(block_count):
            named = routes_ref[0, r] == owner
            live = r < counts_ref[0, 0]
            for k in range(slot_count):
                chosen[k] = jnp.where(named & live & (place == k), r, chosen[k])
            place = place + named.astype(jnp.int32)
        for k in range(slot_count):
            block = jnp.zeros(weighted[0].shape, jnp.float32)
            for r in range(block_count):
                block = jnp.where(chosen[k] == r, weighted[r].astype(jnp.float32), block)
            out_ref[k * block_rows : (k + 1) * block_rows, :] = block.astype(jnp.bfloat16)
        out_ref[slot_count * block_rows :, :] = process_ref[...]


def weigh(design, process, routes, counts, total_slots):
    order = process.shape[1]
    block_count = routes.shape[1]
    block_rows = design.shape[0] // block_count
    rows = block_count // 2 * block_rows + process.shape[0]
    vmem, smem = (pl.BlockSpec(memory_space=m) for m in (pltpu.VMEM, pltpu.SMEM))
    return pl.pallas_call(
        functools.partial(weigh_kernel, total_slots, block_rows),
        out_shape=(jax.ShapeDtypeStruct((rows, order), jnp.bfloat16),) * 2,
        in_specs=[vmem, vmem, smem, smem],
        out_specs=(vmem,) * 2,
    )(design, process, routes, counts)


def first_kernel(times, size, near_ref, sent_ref, prior_ref, out_ref, out_diag_ref, near, far, prior,
                 diag_full, parts, high, low, work, solved_high, solved_low, move_send, move_recv,
                 near_send, near_recv, prior_send, prior_recv, far_send, far_recv):
    place, me, behind, ahead = greet(1, times, size, True)
    rows, order = diag_full.shape[1:]
    observed = near.shape[1] - rows
    piece = near.shape[1] // PIECES
    cuts = [pl.ds(c * piece, piece) for c in range(PIECES)]
    moves = [(sent_ref.at[cut], far.at[place, cut], True) for cut in cuts]
    plan, start, receive, sent = handed(me, 1, behind, ahead, moves, move_send, move_recv)
    start(plan)
    near_spread = Spread(size, place, near, near_send, near_recv, near_ref)
    prior_spread = Spread(size, place, prior, prior_send, prior_recv, prior_ref)
    near_spread.start_own()
    prior_spread.start_own()
    near[place] = near_ref[...]
    prior[place] = prior_ref[...]
    far_spreads = []
    for c, cut in enumerate(cuts):
        receive(plan[c : c + 1])
        far_spreads.append(
            Spread(size, place, far, far_send, far_recv, None, cut, c * (size - 1))
        )
        far_spreads[c].start_own()
    near_spread.forward()
    prior_spread.forward()
    near_spread.finish()
    prior_spread.finish()
    for spread in far_spreads:
        spread.forward()
    square = (rows, rows)
    unit = lax.broadcasted_iota(jnp.int32, square, 0) == lax.broadcasted_iota(jnp.int32, square, 1)

    def add_grams(source):
        for b in range(size):
            cut = slice(b * rows, (b + 1) * rows)
            total = source[b, observed:].astype(jnp.float32)
            for i in range(size):
                total = total + lax.dot_general(
                    source[i, :observed, cut],
                    source[i, :observed, :],
                    (((0,), (0,)), ((), ())),
                    preferred_element_type=jnp.float32,
                )
            yield b, cut, total

    for b, cut, total in add_grams(near):
        diag_full[b] = total
        diag_full[b, :, cut] += jnp.where(unit, jnp.broadcast_to(prior[b][:1], square), 0.0)
        parts[b, 0] = near[b, observed:].astype(jnp.float32)
    for spread in far_spreads:
        spread.finish()
    for b, cut, total in add_grams(far):
        diag_full[b] += total
        for q in range(size):
            turned = far[q, observed:, cut].astype(jnp.float32).T
            parts[b, 1, :, q * rows : (q + 1) * rows] = turned
    out_diag_ref[...] = diag_full[place]
    factor_kernel(diag_full, high, low, work)
    sent(plan)
    put_terms(place, high, low, parts, out_ref, solved_high, solved_low)


def first(near, sent, prior):
    times, size = lax.axis_size("tm"), lax.axis_size("swath")
    order = near.shape[1]
    rows = order // size
    vmem = pl.BlockSpec(memory_space=pltpu.VMEM)
    dma = pltpu.SemaphoreType.DMA
    return pl.pallas_call(
        functools.partial(first_kernel, times, size),
        out_shape=(
            jax.ShapeDtypeStruct((4, rows, order), jnp.float32),
            jax.ShapeDtypeStruct((rows, order), jnp.float32),
        ),
        in_specs=[vmem] * 3,
        out_specs=(vmem,) * 2,
        scratch_shapes=[
            pltpu.VMEM((size,) + near.shape, jnp.bfloat16),
            pltpu.VMEM((size,) + near.shape, jnp.bfloat16),
            pltpu.VMEM((size,) + prior.shape, jnp.float32),
            pltpu.VMEM((size, rows, order), jnp.float32),
            pltpu.VMEM((size, 2, rows, order), jnp.float32),
            pltpu.VMEM((order, order), jnp.bfloat16),
            pltpu.VMEM((order, order), jnp.bfloat16),
            pltpu.VMEM((size, rows, order), jnp.float32),
            pltpu.VMEM((order, 2 * order), jnp.bfloat16),
            pltpu.VMEM((order, 2 * order), jnp.bfloat16),
            dma((PIECES,)),
            dma((PIECES,)),
        ]
        + [dma((size - 1,))] * 4
        + [dma((PIECES * (size - 1),))] * 2,
        compiler_params=pltpu.CompilerParams(collective_id=0, has_side_effects=True),
    )(near, sent, prior)


def shards(design, process, prior_prec, routes, counts):
    row_count = process.shape[1]
    block_count = routes.shape[1]
    block_rows = design.shape[1] // block_count
    total_slots = 2 * (block_count // 2) * block_rows * lax.axis_size("swath")
    near, sent = weigh(design[0], process[0], routes, counts, total_slots)
    prior = jnp.broadcast_to(prior_prec, (8, row_count))
    out, diag_rows = first(near, sent, prior)
    for level in range(1, LEVELS):
        out, diag_rows = step(2 ** (level - 1), out, diag_rows)
    diag_rows, coup_rows = last(2 ** (LEVELS - 1), out, diag_rows)
    return (diag_rows[None], coup_rows[None])


def solution(mesh):
    return jax.shard_map(
        shards,
        mesh=mesh,
        in_specs=(
            P("tm", "swath", None),
            P("tm", "swath", None),
            P("tm", "swath"),
            P("tm", "swath"),
            P("tm", "swath"),
        ),
        out_specs=(P("tm", "swath", None), P("tm", "swath", None)),
        check_vma=False,
    )
```
